256 devices in a mesh: row: 16 (over x_hi, y, core), col: 16 (over z, x_lo).
Axes of the slice: x: 4 (x_hi: 2, x_lo: 2; x = x_hi * 2 + x_lo), y: 4, z: 8, core: 2. Of those that a mesh axis runs over, the one named last changes fastest.
Arguments:
- vectors: float32 [96, 65536], P(None, ('col', 'row')), may hold values from -6 to 6
- blocks: float32 [16, 16, 176, 128, 128], P('row', 'col'), may hold values from -0.0546875 to 0.0546875
- block_row: int32 [16, 16, 176], P('row', 'col'), may hold values from 0 to 31
- block_col: int32 [16, 16, 176], P('row', 'col'), may hold values from 0 to 31
- block_count: int32 [16, 16], P('row', 'col'), may hold values from 22 to 176, as said below
- lower_bound: float32 [1], replicated, may hold values from -2.5 to -1.5
- upper_bound: float32 [1], replicated, may hold values from 1.5 to 2.5
Outputs:
- filtered: float32 [96, 65536], P(None, ('col', 'row'))
The draws below stay inside these ranges and needn't reach their ends.
Inputs may be any that keep to these rules, and one draw needn't show every extreme that they name: `block_row`: local block row index within the device's band. `block_col`: local block column index within the device's band. `block_count`: in every row of the device grid one device has all 176 slots stored.
All inputs are finite; a program needn't handle non-finite values.
Results may differ from the reference program's by a relative error of at most 0.0003.
Values sent between devices are 32-bit elements; how exact they have to be, the bound alone decides.
No kernel may reach another device: no remote copies, remote signals or barrier semaphores. Data moves between devices by JAX's collectives and lax.ppermute only.
A program may use at most 128 MiB of HBM per device.

```python
import jax
import jax.numpy as jnp
from jax import lax

N = 65536
BS = 128
VECS = 96
MAXB = 176
DEGREE = 2
RB = 32
CB = 32
N_ROW = 16
N_COL = 16


def draw_block_count(key, part):
    first_key, second_key = jax.random.split(jax.random.fold_in(key, 17))
    base_count = jax.random.randint(first_key, (N_ROW, N_COL), MAXB // 8, MAXB // 2 + 1)
    full_column = jax.random.randint(second_key, (N_ROW,), 0, N_COL)
    hit_mask = jnp.arange(N_COL)[None, :] == full_column[:, None]
    return jnp.where(hit_mask, MAXB, base_count).astype(jnp.int32)


def set_ends(values, stream_key, least, high):
    index_at = [jax.random.randint(jax.random.fold_in(stream_key, axis), (), 0, length) for axis, length in enumerate(values.shape)]
    main_axis = values.shape.index(max(values.shape))
    neighbour = index_at[:main_axis] + [(index_at[main_axis] + 1) % values.shape[main_axis]] + index_at[main_axis + 1:]
    return values.at[tuple(index_at)].set(least).at[tuple(neighbour)].set(high)


def levels(own_key, shape, shards, low, high):
    def one(axis_at, parts):
        draws = jax.random.uniform(jax.random.fold_in(jax.random.fold_in(own_key, 6), axis_at), (parts,), jnp.float32, low / len(shards), high / len(shards))
        return jnp.repeat(jnp.exp(draws), shape[axis_at] // parts).reshape((-1,) + (1,) * (len(shape) - axis_at - 1))

    factor_of = one(*shards[0])
    for cut in shards[1:]:
        factor_of = factor_of * one(*cut)
    return factor_of


def gaussian(own_key, extent, deviation, most, cuts=(), held_as=jnp.bfloat16):
    values = jax.random.normal(own_key, extent, jnp.float32) * deviation
    if len(cuts) > 0:
        values = levels(own_key, extent, cuts, -0.22, 0.18) * values
    return jnp.clip(values, min=-most, max=most).astype(held_as)


def setup_inputs(seed: int = 0) -> dict:
    streams_of = jax.random.split(jax.random.key(seed), 8)
    return {
        "vectors": gaussian(streams_of[0], (VECS, N), 1.0, 6.0, ((1, 256),), jnp.float32),
        "blocks": gaussian(streams_of[1], (N_ROW, N_COL, MAXB, BS, BS), (MAXB * N_ROW * N_COL * BS * BS // N) ** -0.5, 0.0546875, ((0, 16), (1, 16)), jnp.float32),
        "block_row": set_ends(jax.random.randint(streams_of[2], (N_ROW, N_COL, MAXB), 0, RB), jax.random.fold_in(streams_of[2], 1), 0, RB - 1).astype(jnp.int32),
        "block_col": set_ends(jax.random.randint(streams_of[3], (N_ROW, N_COL, MAXB), 0, CB), jax.random.fold_in(streams_of[3], 1), 0, CB - 1).astype(jnp.int32),
        "block_count": draw_block_count(jax.random.fold_in(streams_of[7], 71), 0),
        "lower_bound": jnp.clip(jax.random.uniform(streams_of[5], (1,), jnp.float32, -2.5, -1.5), -2.5, -1.5),
        "upper_bound": jnp.clip(jax.random.uniform(streams_of[6], (1,), jnp.float32, 1.5, 2.5), 1.5, 2.5),
    }


def hamiltonian_product(vectors, blocks, block_row, block_col, block_count):
    block_total = N // BS
    vec_blocks = vectors.reshape(VECS, block_total, BS)
    flat_blocks = blocks.reshape(N_ROW * N_COL, MAXB, BS, BS)
    flat_rows = block_row.reshape(N_ROW * N_COL, MAXB)
    flat_cols = block_col.reshape(N_ROW * N_COL, MAXB)
    flat_count = block_count.reshape(N_ROW * N_COL)
    device_ids = jnp.arange(N_ROW * N_COL, dtype=jnp.int32)

    def visit_device(accumulated, inputs):
        device_blocks, rows_local, cols_local, slot_count, device_id = inputs
        global_row = (device_id // N_COL) * RB + rows_local
        global_col = (device_id % N_COL) * CB + cols_local
        live_mask = (jnp.arange(MAXB) < slot_count).astype(jnp.float32)
        source_col = jnp.take(vec_blocks, global_col, axis=1)
        forward = jnp.einsum("sij,vsj->vsi", device_blocks, source_col, precision=lax.Precision.HIGHEST)
        forward = forward * live_mask[None, :, None]
        source_row = jnp.take(vec_blocks, global_row, axis=1)
        backward = jnp.einsum("sij,vsi->vsj", device_blocks, source_row, precision=lax.Precision.HIGHEST)
        backward = backward * live_mask[None, :, None]
        accumulated = accumulated.at[:, global_row].add(forward)
        accumulated = accumulated.at[:, global_col].add(backward)
        return accumulated, None

    start = jnp.zeros((VECS, block_total, BS), jnp.float32)
    result, _ = lax.scan(visit_device, start, (flat_blocks, flat_rows, flat_cols, flat_count, device_ids))
    return result.reshape(VECS, N)


def reference(vectors, blocks, block_row, block_col, block_count, lower_bound, upper_bound):
    center = (upper_bound[0] + lower_bound[0]) / 2.0
    half_width = (upper_bound[0] - lower_bound[0]) / 2.0
    previous = vectors
    current = (hamiltonian_product(vectors, blocks, block_row, block_col, block_count) - center * vectors) / half_width
    for iteration in range(DEGREE - 1):
        product = hamiltonian_product(current, blocks, block_row, block_col, block_count)
        following = 2.0 * (product - center * current) / half_width - previous
        previous, current = current, following
    return current
```

```python
import functools

import jax
import jax.numpy as jnp
from jax import lax
from jax.experimental import pallas as pl
from jax.experimental.pallas import tpu as pltpu
from jax.sharding import PartitionSpec as P

f32, bf16 = jnp.float32, jnp.bfloat16

NX, NY, NC, NZ, NL = 2, 4, 2, 8, 2


def row_perm(f):
    def at(x, y, c):
        return ((x % NX) * NY + y % NY) * NC + c % NC

    return [(at(x, y, c), at(*f(x, y, c))) for x in range(NX) for y in range(NY) for c in range(NC)]


def col_perm(f):
    def at(z, l):
        return (z % NZ) * NL + l % NL

    return [(at(z, l), at(*f(z, l))) for z in range(NZ) for l in range(NL)]


CORE = row_perm(lambda x, y, c: (x, y, c + 1))
Y_UP = row_perm(lambda x, y, c: (x, y + 1, c))
Y_DOWN = row_perm(lambda x, y, c: (x, y - 1, c))
X_HI = row_perm(lambda x, y, c: (x + 1, y, c))
Z_UP = col_perm(lambda z, l: (z + 1, l))
Z_DOWN = col_perm(lambda z, l: (z - 1, l))
X_LO = col_perm(lambda z, l: (z, l + 1))
FLIP = [(i * 16 + j, j * 16 + i) for i in range(16) for j in range(16)]


def send(x, axis, perm):
    return lax.ppermute(x, axis, perm)


def flip(x):
    return lax.ppermute(x, ("row", "col"), FLIP)


def cat(*xs):
    return jnp.concatenate(xs, axis=0)


def gather_row(a0):
    a1 = send(a0, "row", X_HI)
    p0 = cat(a0, a1)
    up = send(p0, "row", Y_DOWN)
    down = send(p0, "row", Y_UP)
    q0 = send(p0, "row", CORE)
    far_a = send(down[:2], "row", Y_UP)
    far_b = send(up[2:], "row", Y_DOWN)
    qu = send(up, "row", CORE)
    qd = send(down, "row", CORE)
    qa = send(far_a, "row", CORE)
    qb = send(far_b, "row", CORE)
    return [p0, up, far_a, far_b, down, q0, qu, qa, qb, qd]


def gather_col(t0):
    t1 = send(t0, "col", X_LO)
    up, down, ups, downs = cat(t0, t1), None, [], []
    own = up
    up, down = own, own
    for _ in range(3):
        up = send(up, "col", Z_DOWN)
        down = send(down, "col", Z_UP)
        ups.append(up)
        downs.append(down)
    far_a = send(down[:2], "col", Z_UP)
    far_b = send(up[2:], "col", Z_DOWN)
    return [own] + ups + [far_a, far_b] + downs[::-1]


def scatter_col(parts):
    f0, f1, f2, f3, f4a, f4b, f5, f6, f7 = parts
    up = send(f4a, "col", Z_UP)
    down = send(f4b, "col", Z_DOWN)
    up = send(cat(f3[:2] + up, f3[2:]), "col", Z_UP)
    down = send(cat(f5[:2], f5[2:] + down), "col", Z_DOWN)
    up = send(f2 + up, "col", Z_UP)
    down = send(f6 + down, "col", Z_DOWN)
    up = send(f1 + up, "col", Z_UP)
    down = send(f7 + down, "col", Z_DOWN)
    other = send(f0[2:] + up[2:] + down[2:], "col", X_LO)
    return f0[:2] + up[:2] + down[:2] + other


def scatter_row(parts):
    g0, g1, g2a, g2b, g3, other = parts
    o = send(other, "row", CORE)
    up = send(g2a + o[8:10], "row", Y_UP)
    down = send(g2b + o[10:12], "row", Y_DOWN)
    up = send(cat(g1[:2] + o[4:6] + up, g1[2:] + o[6:8]), "row", Y_UP)
    down = send(cat(g3[:2] + o[12:14], g3[2:] + o[14:16] + down), "row", Y_DOWN)
    last = send(g0[2:] + o[2:4] + up[2:] + down[2:], "row", X_HI)
    return g0[:2] + o[:2] + up[:2] + down[:2] + last


COL_PARTS = (4, 4, 2, 2, 4, 4, 4, 2, 2, 4)
ROW_PARTS = (4, 4, 4, 4, 2, 2, 4, 4, 4)
OUT_FORWARD = (4, 4, 4, 4, 2, 2, 4, 4, 4)
OUT_BACKWARD = (4, 4, 2, 2, 4, 16)


def split(x):
    high = x.astype(bf16)
    return high, (x - high.astype(f32)).astype(bf16)


def col_slot(cb, row):
    i = cb >> 1
    core = (i ^ row) & 1
    y = ((i >> 1) - (row >> 1)) & 3
    x = ((i >> 3) ^ (row >> 3)) & 1
    return (((core * 4 + y) * 2 + x) << 1) + (cb & 1)


def row_slot(rb, col):
    i = rb >> 1
    z = ((i >> 1) - (col >> 1)) & 7
    l = (i ^ col) & 1
    return ((z * 2 + l) << 1) + (rb & 1)


def product_kernel(backward, in_sizes, out_sizes, unroll, *refs):
    rows, cols, count, here = refs[:4]
    parts = refs[4 : 4 + len(in_sizes)]
    blocks = refs[4 + len(in_sizes)]
    outs = refs[5 + len(in_sizes) : 5 + len(in_sizes) + len(out_sizes)]
    halves, total, held, sems = refs[5 + len(in_sizes) + len(out_sizes) :]
    live = count[0, 0]
    chunks = lax.div(live + unroll - 1, unroll)
    bs = blocks.shape[-1]

    def copy(c):
        where = pl.ds(c * unroll, unroll)
        return pltpu.make_async_copy(blocks.at[0, 0, where], held.at[where], sems.at[c])

    @pl.loop(0, chunks)
    def _(c):
        copy(c).start()

    offset = 0
    for part, size in zip(parts, in_sizes):
        for k in range(size):
            high, low = split(part[k])
            halves[offset + k, :, :bs] = high
            halves[offset + k, :, bs:] = low
        offset += size
    total[...] = jnp.zeros_like(total)
    row, col = here[0], here[1]

    def one(s):
        rb, cb = row_slot(rows[0, 0, s], col), col_slot(cols[0, 0, s], row)
        high, low = split(held[s])
        zero = jnp.zeros_like(low)
        if backward:
            weights = jnp.concatenate(
                [jnp.concatenate([high, low], 1), jnp.concatenate([high, zero], 1)], 0
            )
            out = jnp.dot(halves[rb], weights, preferred_element_type=f32)
            total[cb] += out[:, :bs] + out[:, bs:]
        else:
            weights = jnp.concatenate(
                [jnp.concatenate([high, high], 1), jnp.concatenate([low, zero], 1)], 0
            )
            out = lax.dot_general(
                halves[cb], weights, (((1,), (1,)), ((), ())), preferred_element_type=f32
            )
            total[rb] += out[:, :bs] + out[:, bs:]

    full = lax.div(live, unroll)

    @pl.loop(0, full)
    def _(c):
        copy(c).wait()
        for k in range(unroll):
            one(c * unroll + k)

    @pl.when(full < chunks)
    def _():
        copy(full).wait()

        @pl.loop(full * unroll, live)
        def _(s):
            one(s)

    offset = 0
    for out, size in zip(outs, out_sizes):
        out[...] = total[offset : offset + size]
        offset += size


def products(backward, parts, blocks, rows, cols, count, here):
    in_sizes = ROW_PARTS if backward else COL_PARTS
    out_sizes = OUT_BACKWARD if backward else OUT_FORWARD
    slots, bs = blocks.shape[2], blocks.shape[-1]
    vecs = parts[0].shape[1]
    unroll = 16
    smem = pl.BlockSpec(memory_space=pltpu.SMEM)
    vmem = pl.BlockSpec(memory_space=pltpu.VMEM)
    return pl.pallas_call(
        functools.partial(product_kernel, backward, in_sizes, out_sizes, unroll),
        in_specs=[smem] * 4 + [vmem] * len(parts) + [pl.BlockSpec(memory_space=pl.ANY)],
        out_specs=[vmem] * len(out_sizes),
        out_shape=[jax.ShapeDtypeStruct((n, vecs, bs), f32) for n in out_sizes],
        scratch_shapes=[
            pltpu.VMEM((sum(in_sizes), vecs, 2 * bs), bf16),
            pltpu.VMEM((sum(out_sizes), vecs, bs), f32),
            pltpu.VMEM((slots, bs, bs), f32),
            pltpu.SemaphoreType.DMA((slots // unroll,)),
        ],
        compiler_params=pltpu.CompilerParams(vmem_limit_bytes=32 << 20),
        cost_estimate=pl.CostEstimate(
            flops=8 * slots * vecs * bs * bs, bytes_accessed=4 * slots * bs * bs, transcendentals=0
        ),
        name="backward" if backward else "forward",
    )(rows, cols, count, here, *parts, blocks)


def body(vectors, blocks, block_row, block_col, block_count, lower_bound, upper_bound):
    vecs, bs = vectors.shape[0], blocks.shape[-1]
    here = jnp.stack([lax.axis_index("row"), lax.axis_index("col")]).astype(jnp.int32)
    center = (upper_bound[0] + lower_bound[0]) / 2.0
    half_width = (upper_bound[0] - lower_bound[0]) / 2.0
    index = (blocks, block_row, block_col, block_count, here)

    def apply_hamiltonian(own, flipped):
        forward = products(False, gather_row(own), *index)
        backward = products(True, gather_col(flipped), *index)
        return scatter_row(backward), scatter_col(forward)

    y0 = vectors.reshape(vecs, -1, bs).transpose(1, 0, 2)
    y0_flipped = flip(y0)
    own, flipped = apply_hamiltonian(y0, y0_flipped)
    y1 = (own + flip(flipped) - center * y0) / half_width
    y1_flipped = (flipped + flip(own) - center * y0_flipped) / half_width
    own, flipped = apply_hamiltonian(y1, y1_flipped)
    y2 = 2.0 * (own + flip(flipped) - center * y1) / half_width - y0
    return y2.transpose(1, 0, 2).reshape(vectors.shape)


def solution(mesh):
    placed = (
        P(None, ("col", "row")),
        P("row", "col", None, None, None),
        P("row", "col", None),
        P("row", "col", None),
        P("row", "col"),
        P(),
        P(),
    )
    return jax.shard_map(
        body, mesh=mesh, in_specs=placed, out_specs=P(None, ("col", "row")), check_vma=False
    )
```

```python
import functools

import jax
import jax.numpy as jnp
from jax import lax
from jax.experimental import pallas as pl
from jax.experimental.pallas import tpu as pltpu
from jax.sharding import PartitionSpec as P

f32, bf16 = jnp.float32, jnp.bfloat16

NX, NY, NC, NZ, NL = 2, 4, 2, 8, 2


def row_perm(f):
    def at(x, y, c):
        return ((x % NX) * NY + y % NY) * NC + c % NC

    return [(at(x, y, c), at(*f(x, y, c))) for x in range(NX) for y in range(NY) for c in range(NC)]


def col_perm(f):
    def at(z, l):
        return (z % NZ) * NL + l % NL

    return [(at(z, l), at(*f(z, l))) for z in range(NZ) for l in range(NL)]


CORE = row_perm(lambda x, y, c: (x, y, c + 1))
Y_UP = row_perm(lambda x, y, c: (x, y + 1, c))
Y_DOWN = row_perm(lambda x, y, c: (x, y - 1, c))
Y_FAR = row_perm(lambda x, y, c: (x, y + 2, c))
X_HI = row_perm(lambda x, y, c: (x + 1, y, c))
Z_UP = col_perm(lambda z, l: (z + 1, l))
Z_DOWN = col_perm(lambda z, l: (z - 1, l))
X_LO = col_perm(lambda z, l: (z, l + 1))
FLIP = [(i * 16 + j, j * 16 + i) for i in range(16) for j in range(16)]


def send(x, axis, perm):
    return lax.ppermute(x, axis, perm)


def flip(x):
    return lax.ppermute(x, ("row", "col"), FLIP)


def cat(*xs):
    return jnp.concatenate(xs, axis=0)


def bar(*xs):
    return lax.optimization_barrier(xs)


FORWARD_OUT = (4, 4, 4, 4, 2, 2, 4, 4, 4)
ROW_PARTS = (4, 4, 4, 4, 2, 2, 4, 4, 4)
BACKWARD_OUT = (4, 4, 4, 4, 16)


def split(x):
    high = x.astype(bf16)
    return high, (x - high.astype(f32)).astype(bf16)


def col_slot(cb, row):
    i = cb >> 1
    core = (i ^ row) & 1
    y = ((i >> 1) - (row >> 1)) & 3
    x = ((i >> 3) ^ (row >> 3)) & 1
    return (((core * 4 + y) * 2 + x) << 1) + (cb & 1)


def row_slot(rb, col):
    i = rb >> 1
    z = ((i >> 1) - (col >> 1)) & 7
    l = (i ^ col) & 1
    return ((z * 2 + l) << 1) + (rb & 1)


def product_kernel(backward, first, last, in_sizes, out_sizes, *refs):
    rows, cols, count, here, blocks = refs[:5]
    parts, refs = refs[5 : 5 + len(in_sizes)], refs[5 + len(in_sizes) :]
    if not first:
        halves, total_in, refs = refs[0], refs[1], refs[2:]
    outs, refs = refs[: len(out_sizes)], refs[len(out_sizes) :]
    if first:
        halves, total, held, sems = refs
    else:
        total, held, sems = refs
    live = count[0, 0]
    bs = blocks.shape[-1]
    full = lax.div(live, UNROLL)
    middle = lax.div(full, 2)
    begin = 0 if first else middle
    end = full if last else middle

    def copy(c):
        where = pl.ds(c * UNROLL, UNROLL)
        return pltpu.make_async_copy(blocks.at[0, 0, where], held.at[where], sems.at[c])

    @pl.loop(begin, end)
    def _(c):
        copy(c).start()

    if last:

        @pl.when(full * UNROLL < live)
        def _():
            copy(full).start()

    if first:
        offset = 0
        for part, size in zip(parts, in_sizes):
            @pl.loop(0, size)
            def _(k, part=part, offset=offset):
                high, low = split(part[k])
                halves[offset + k, :, :bs] = high
                halves[offset + k, :, bs:] = low

            offset += size
        total[...] = jnp.zeros_like(total)
    else:
        total[...] = total_in[...]
    row, col = here[0], here[1]

    def one(s):
        rb, cb = row_slot(rows[0, 0, s], col), col_slot(cols[0, 0, s], row)
        high, low = split(held[s])
        zero = jnp.zeros_like(low)
        if backward:
            weights = jnp.concatenate(
                [jnp.concatenate([high, low], 1), jnp.concatenate([high, zero], 1)], 0
            )
            out = jnp.dot(halves[rb], weights, preferred_element_type=f32)
            total[cb] += out[:, :bs] + out[:, bs:]
        else:
            weights = jnp.concatenate(
                [jnp.concatenate([high, high], 1), jnp.concatenate([low, zero], 1)], 0
            )
            out = lax.dot_general(
                halves[cb], weights, (((1,), (1,)), ((), ())), preferred_element_type=f32
            )
            total[rb] += out[:, :bs] + out[:, bs:]

    @pl.loop(begin, end)
    def _(c):
        copy(c).wait()
        for k in range(UNROLL):
            one(c * UNROLL + k)

    if last:

        @pl.when(full * UNROLL < live)
        def _():
            copy(full).wait()

            @pl.loop(full * UNROLL, live)
            def _(s):
                one(s)

        offset = 0
        for out, size in zip(outs, out_sizes):
            out[...] = total[offset : offset + size]
            offset += size


UNROLL = 16


def products(backward, first, last, state, index):
    blocks = index[4]
    slots, bs = blocks.shape[2], blocks.shape[-1]
    vecs = state[0].shape[1]
    in_sizes = () if not first else ROW_PARTS if backward else (4,) * 8
    out_sizes = () if not last else BACKWARD_OUT if backward else FORWARD_OUT
    smem = pl.BlockSpec(memory_space=pltpu.SMEM)
    vmem = pl.BlockSpec(memory_space=pltpu.VMEM)
    halves, total = (32, vecs, 2 * bs), (32, vecs, bs)
    out_shape = [jax.ShapeDtypeStruct((n, vecs, bs), f32) for n in out_sizes]
    scratch = []
    if first and not last:
        out_shape += [jax.ShapeDtypeStruct(halves, bf16), jax.ShapeDtypeStruct(total, f32)]
    elif first:
        scratch = [pltpu.VMEM(halves, bf16), pltpu.VMEM(total, f32)]
    else:
        scratch = [pltpu.VMEM(total, f32)]
    scratch += [
        pltpu.VMEM((slots, bs, bs), f32),
        pltpu.SemaphoreType.DMA((slots // UNROLL,)),
    ]
    share = 1 if first and last else 2
    return pl.pallas_call(
        functools.partial(product_kernel, backward, first, last, in_sizes, out_sizes),
        in_specs=[smem] * 4 + [pl.BlockSpec(memory_space=pltpu.HBM)] + [vmem] * len(state),
        out_specs=[vmem] * len(out_shape),
        out_shape=out_shape,
        scratch_shapes=scratch,
        compiler_params=pltpu.CompilerParams(vmem_limit_bytes=48 << 20),
        cost_estimate=pl.CostEstimate(
            flops=24 * slots * vecs * bs * bs // share,
            bytes_accessed=4 * slots * bs * bs // share,
            transcendentals=0,
        ),
        name=("backward" if backward else "forward") + str(int(first) + 2 * int(last)),
    )(*index, *state)


def body(vectors, blocks, block_row, block_col, block_count, lower_bound, upper_bound):
    vecs, bs = vectors.shape[0], blocks.shape[-1]
    here = jnp.stack([lax.axis_index("row"), lax.axis_index("col")]).astype(jnp.int32)
    center = (upper_bound[0] + lower_bound[0]) / 2.0
    half_width = (upper_bound[0] - lower_bound[0]) / 2.0
    index = (block_row, block_col, block_count, here, blocks)

    def apply_hamiltonian(a0, flipping, finish):
        a1 = send(a0, "row", X_HI)
        _, flipping = bar(a1, flipping)
        p0 = cat(a0, a1)
        p1 = send(p0, "row", Y_DOWN)
        p2 = send(p0, "row", Y_FAR)
        p3 = send(p0, "row", Y_UP)
        c0 = send(p0, "row", CORE)
        t0 = finish(flipping)
        t1 = send(t0, "col", X_LO)
        p1, p2, p3, t0, t1, c0 = bar(p1, p2, p3, t0, t1, c0)
        z0 = cat(t0, t1)
        up1 = send(z0, "col", Z_DOWN)
        down1 = send(z0, "col", Z_UP)
        c1, c2, c3 = (send(p, "row", CORE) for p in (p1, p2, p3))
        state = products(False, True, False, (p0, p1, p2, p3, c0, c1, c2, c3), index)
        up1, down1, *state = bar(up1, down1, *state)
        up2 = send(up1, "col", Z_DOWN)
        down2 = send(down1, "col", Z_UP)
        forward = products(False, False, True, state, index)
        up2, down2, *forward = bar(up2, down2, *forward)
        f0, f1, f2, f3, f4a, f4b, f5, f6, f7 = forward
        up3 = send(up2, "col", Z_DOWN)
        down3 = send(down2, "col", Z_UP)
        u = send(f4a, "col", Z_UP)
        d = send(f4b, "col", Z_DOWN)
        up3, down3, u, d = bar(up3, down3, u, d)
        far_a = send(down3[:2], "col", Z_UP)
        far_b = send(up3[2:], "col", Z_DOWN)
        u = send(cat(f3[:2] + u, f3[2:]), "col", Z_UP)
        d = send(cat(f5[:2], f5[2:] + d), "col", Z_DOWN)
        far_a, far_b, u, d = bar(far_a, far_b, u, d)
        u = send(f2 + u, "col", Z_UP)
        d = send(f6 + d, "col", Z_DOWN)
        state = (z0, up1, up2, up3, far_a, far_b, down3, down2, down1)
        backward = products(True, True, True, state, index)
        u, d, *backward = bar(u, d, *backward)
        g0, g1, g2, g3, other = backward
        u = send(f1 + u, "col", Z_UP)
        d = send(f7 + d, "col", Z_DOWN)
        o = send(other, "row", CORE)
        u, d, o = bar(u, d, o)
        h = send(f0[2:] + u[2:] + d[2:], "col", X_LO)
        q1 = send(g1 + o[4:8], "row", Y_UP)
        q2 = send(g2 + o[8:12], "row", Y_FAR)
        q3 = send(g3 + o[12:], "row", Y_DOWN)
        (flipped,) = bar(f0[:2] + u[:2] + d[:2] + h)
        last = send(g0[2:] + o[2:4] + q1[2:] + q2[2:] + q3[2:], "row", X_HI)
        (own,) = bar(g0[:2] + o[:2] + q1[:2] + q2[:2] + q3[:2] + last)
        return own, flipped, t0

    y0 = vectors.reshape(vecs, -1, bs).transpose(1, 0, 2)
    own, flipped, y0_flipped = apply_hamiltonian(y0, flip(y0), lambda x: x)
    own_flipping = flip(own)
    y1 = (own + flip(flipped) - center * y0) / half_width
    own, flipped, _ = apply_hamiltonian(
        y1, own_flipping, lambda x: (flipped + x - center * y0_flipped) / half_width
    )
    y2 = 2.0 * (own + flip(flipped) - center * y1) / half_width - y0
    return y2.transpose(1, 0, 2).reshape(vectors.shape)


def solution(mesh):
    placed = (
        P(None, ("col", "row")),
        P("row", "col", None, None, None),
        P("row", "col", None),
        P("row", "col", None),
        P("row", "col"),
        P(),
        P(),
    )
    return jax.shard_map(
        body, mesh=mesh, in_specs=placed, out_specs=P(None, ("col", "row")), check_vma=False
    )
```

```python
import functools

import jax
import jax.numpy as jnp
from jax import lax
from jax.experimental import pallas as pl
from jax.experimental.pallas import tpu as pltpu
from jax.sharding import PartitionSpec as P


f32, bf16 = jnp.float32, jnp.bfloat16

NX, NY, NC, NZ, NL = 2, 4, 2, 8, 2


def row_perm(f):
    def at(x, y, c):
        return ((x % NX) * NY + y % NY) * NC + c % NC

    return [(at(x, y, c), at(*f(x, y, c))) for x in range(NX) for y in range(NY) for c in range(NC)]


def col_perm(f):
    def at(z, l):
        return (z % NZ) * NL + l % NL

    return [(at(z, l), at(*f(z, l))) for z in range(NZ) for l in range(NL)]


CORE = row_perm(lambda x, y, c: (x, y, c + 1))
Y_UP = row_perm(lambda x, y, c: (x, y + 1, c))
Y_DOWN = row_perm(lambda x, y, c: (x, y - 1, c))
Y_FAR = row_perm(lambda x, y, c: (x, y + 2, c))
X_HI = row_perm(lambda x, y, c: (x + 1, y, c))
Z_UP = col_perm(lambda z, l: (z + 1, l))
Z_DOWN = col_perm(lambda z, l: (z - 1, l))
X_LO = col_perm(lambda z, l: (z, l + 1))
FLIP = [(i * 16 + j, j * 16 + i) for i in range(16) for j in range(16)]


def send(x, axis, perm):
    return lax.ppermute(x, axis, perm)


def flip(x):
    return lax.ppermute(x, ("row", "col"), FLIP)


def cat(*xs):
    return jnp.concatenate(xs, axis=0)


def bar(*xs):
    return lax.optimization_barrier(xs)


FORWARD_OUT = (4, 4, 4, 4, 2, 2, 4, 4, 4)
BACKWARD_OUT = (4, 4, 4, 4, 16)
FORWARD_IN = ((0, 0, 16), (1, 0, 16))
BACKWARD_IN = (
    (0, 0, 4), (1, 0, 4), (2, 0, 4), (3, 0, 4), (4, 0, 2), (5, 0, 2), (6, 0, 4), (7, 0, 4), (8, 0, 4)
)


def split(x):
    high = x.astype(bf16)
    return high, (x - high.astype(f32)).astype(bf16)


def col_slot(cb, row):
    i = cb >> 1
    core = (i ^ row) & 1
    y = ((i >> 1) - (row >> 1)) & 3
    x = ((i >> 3) ^ (row >> 3)) & 1
    return (((core * 4 + y) * 2 + x) << 1) + (cb & 1)


def row_slot(rb, col):
    i = rb >> 1
    z = ((i >> 1) - (col >> 1)) & 7
    l = (i ^ col) & 1
    return ((z * 2 + l) << 1) + (rb & 1)


def product_kernel(backward, first, last, n_in, runs, out_sizes, *refs):
    rows, cols, count, here, blocks = refs[:5]
    parts, refs = refs[5 : 5 + n_in], refs[5 + n_in :]
    if not first:
        halves, total_in, refs = refs[0], refs[1], refs[2:]
    outs, refs = refs[: len(out_sizes)], refs[len(out_sizes) :]
    if first:
        halves, total, held, sems = refs
    else:
        total, held, sems = refs
    live = count[0, 0]
    bs = blocks.shape[-1]
    full = lax.div(live, UNROLL)
    middle = lax.div(full, 2)
    begin = 0 if first else middle
    end = full if last else middle

    def copy(c):
        where = pl.ds(c * UNROLL, UNROLL)
        return pltpu.make_async_copy(blocks.at[0, 0, where], held.at[where], sems.at[c])

    @pl.loop(begin, end)
    def _(c):
        copy(c).start()

    if last:

        @pl.when(full * UNROLL < live)
        def _():
            copy(full).start()

    if first:
        offset = 0
        for array, at, size in runs:

            @pl.loop(0, size)
            def _(k, part=parts[array], at=at, offset=offset):
                high, low = split(part[at + k])
                halves[offset + k, :, :bs] = high
                halves[offset + k, :, bs:] = low

            offset += size
        total[...] = jnp.zeros_like(total)
    else:
        total[...] = total_in[...]
    row, col = here[0], here[1]

    def one(s):
        rb, cb = row_slot(rows[0, 0, s], col), col_slot(cols[0, 0, s], row)
        high, low = split(held[s])
        zero = jnp.zeros_like(low)
        if backward:
            weights = jnp.concatenate(
                [jnp.concatenate([high, low], 1), jnp.concatenate([high, zero], 1)], 0
            )
            out = jnp.dot(halves[rb], weights, preferred_element_type=f32)
            total[cb] += out[:, :bs] + out[:, bs:]
        else:
            weights = jnp.concatenate(
                [jnp.concatenate([high, high], 1), jnp.concatenate([low, zero], 1)], 0
            )
            out = lax.dot_general(
                halves[cb], weights, (((1,), (1,)), ((), ())), preferred_element_type=f32
            )
            total[rb] += out[:, :bs] + out[:, bs:]

    @pl.loop(begin, end)
    def _(c):
        copy(c).wait()
        for k in range(UNROLL):
            one(c * UNROLL + k)

    if last:

        @pl.when(full * UNROLL < live)
        def _():
            copy(full).wait()

            @pl.loop(full * UNROLL, live)
            def _(s):
                one(s)

        offset = 0
        for out, size in zip(outs, out_sizes):
            out[...] = total[offset : offset + size]
            offset += size


UNROLL = 16


def products(backward, first, last, state, index):
    blocks = index[4]
    slots, bs = blocks.shape[2], blocks.shape[-1]
    vecs = state[0].shape[1]
    n_in = len(state) if first else 0
    runs = BACKWARD_IN if backward else FORWARD_IN
    out_sizes = () if not last else BACKWARD_OUT if backward else FORWARD_OUT
    smem = pl.BlockSpec(memory_space=pltpu.SMEM)
    vmem = pl.BlockSpec(memory_space=pltpu.VMEM)
    halves, total = (32, vecs, 2 * bs), (32, vecs, bs)
    out_shape = [jax.ShapeDtypeStruct((n, vecs, bs), f32) for n in out_sizes]
    scratch = []
    if first and not last:
        out_shape += [jax.ShapeDtypeStruct(halves, bf16), jax.ShapeDtypeStruct(total, f32)]
    elif first:
        scratch = [pltpu.VMEM(halves, bf16), pltpu.VMEM(total, f32)]
    else:
        scratch = [pltpu.VMEM(total, f32)]
    scratch += [
        pltpu.VMEM((slots, bs, bs), f32),
        pltpu.SemaphoreType.DMA((slots // UNROLL,)),
    ]
    share = 1 if first and last else 2
    return pl.pallas_call(
        functools.partial(product_kernel, backward, first, last, n_in, runs, out_sizes),
        in_specs=[smem] * 4 + [pl.BlockSpec(memory_space=pltpu.HBM)] + [vmem] * len(state),
        out_specs=[vmem] * len(out_shape),
        out_shape=out_shape,
        scratch_shapes=scratch,
        compiler_params=pltpu.CompilerParams(vmem_limit_bytes=48 << 20),
        cost_estimate=pl.CostEstimate(
            flops=24 * slots * vecs * bs * bs // share,
            bytes_accessed=4 * slots * bs * bs // share,
            transcendentals=0,
        ),
    )(*index, *state)


def body(vectors, blocks, block_row, block_col, block_count, lower_bound, upper_bound):
    vecs, bs = vectors.shape[0], blocks.shape[-1]
    here = jnp.stack([lax.axis_index("row"), lax.axis_index("col")]).astype(jnp.int32)
    center = (upper_bound[0] + lower_bound[0]) / 2.0
    half_width = (upper_bound[0] - lower_bound[0]) / 2.0
    index = (block_row, block_col, block_count, here, blocks)

    def apply_hamiltonian(a0, flipping, finish):
        a1 = send(a0, "row", X_HI)
        _, flipping = bar(a1, flipping)
        p0 = cat(a0, a1)
        p1 = send(p0, "row", Y_DOWN)
        p2 = send(p0, "row", Y_FAR)
        p3 = send(p0, "row", Y_UP)
        t0 = finish(flipping)
        t1 = send(t0, "col", X_LO)
        p1, p2, p3, t0, t1 = bar(p1, p2, p3, t0, t1)
        z0 = cat(t0, t1)
        up1 = send(z0, "col", Z_DOWN)
        down1 = send(z0, "col", Z_UP)
        p = cat(p0, p1, p2, p3)
        state = products(False, True, False, (p, send(p, "row", CORE)), index)
        up1, down1, *state = bar(up1, down1, *state)
        up2 = send(up1, "col", Z_DOWN)
        down2 = send(down1, "col", Z_UP)
        forward = products(False, False, True, state, index)
        up2, down2, *forward = bar(up2, down2, *forward)
        f0, f1, f2, f3, f4a, f4b, f5, f6, f7 = forward
        up3 = send(cat(up2, f4b), "col", Z_DOWN)
        down3 = send(cat(down2, f4a), "col", Z_UP)
        up3, down3 = bar(up3, down3)
        up4 = send(cat(up3[2:4], f5[:2], f5[2:] + up3[4:]), "col", Z_DOWN)
        down4 = send(cat(down3[:2], f3[:2] + down3[4:], f3[2:]), "col", Z_UP)
        up4, down4 = bar(up4, down4)
        u = send(f2 + down4[2:], "col", Z_UP)
        d = send(f6 + up4[2:], "col", Z_DOWN)
        state = (z0, up1, up2, up3, down4, up4, down3, down2, down1)
        backward = products(True, True, True, state, index)
        u, d, *backward = bar(u, d, *backward)
        g0, g1, g2, g3, other = backward
        u = send(f1 + u, "col", Z_UP)
        d = send(f7 + d, "col", Z_DOWN)
        o = send(other, "row", CORE)
        u, d, o = bar(u, d, o)
        h = send(f0[2:] + u[2:] + d[2:], "col", X_LO)
        q1 = send(g1 + o[4:8], "row", Y_UP)
        q2 = send(g2 + o[8:12], "row", Y_FAR)
        q3 = send(g3 + o[12:], "row", Y_DOWN)
        (flipped,) = bar(f0[:2] + u[:2] + d[:2] + h)
        flipped_back = flip(flipped)
        last = send(g0[2:] + o[2:4] + q1[2:] + q2[2:] + q3[2:], "row", X_HI)
        (own,) = bar(g0[:2] + o[:2] + q1[:2] + q2[:2] + q3[:2] + last)
        return own, flipped, flipped_back, t0

    y0 = vectors.reshape(vecs, -1, bs).transpose(1, 0, 2)
    own, flipped, flipped_back, y0_flipped = apply_hamiltonian(y0, flip(y0), lambda x: x)
    own_flipping = flip(own)
    y1 = (own + flipped_back - center * y0) / half_width
    own, flipped, flipped_back, _ = apply_hamiltonian(
        y1, own_flipping, lambda x: (flipped + x - center * y0_flipped) / half_width
    )
    y2 = 2.0 * (own + flipped_back - center * y1) / half_width - y0
    return y2.transpose(1, 0, 2).reshape(vectors.shape)


def solution(mesh):
    placed = (
        P(None, ("col", "row")),
        P("row", "col", None, None, None),
        P("row", "col", None),
        P("row", "col", None),
        P("row", "col"),
        P(),
        P(),
    )
    return jax.shard_map(
        body, mesh=mesh, in_specs=placed, out_specs=P(None, ("col", "row")), check_vma=False
    )
```

```python
import functools

import jax
import jax.numpy as jnp
from jax import lax
from jax.experimental import pallas as pl
from jax.experimental.pallas import tpu as pltpu
from jax.sharding import PartitionSpec as P


f32, bf16 = jnp.float32, jnp.bfloat16

NX, NY, NC, NZ, NL = 2, 4, 2, 8, 2


def row_perm(f):
    def at(x, y, c):
        return ((x % NX) * NY + y % NY) * NC + c % NC

    return [(at(x, y, c), at(*f(x, y, c))) for x in range(NX) for y in range(NY) for c in range(NC)]


def col_perm(f):
    def at(z, l):
        return (z % NZ) * NL + l % NL

    return [(at(z, l), at(*f(z, l))) for z in range(NZ) for l in range(NL)]


CORE = row_perm(lambda x, y, c: (x, y, c + 1))
Y_UP = row_perm(lambda x, y, c: (x, y + 1, c))
Y_DOWN = row_perm(lambda x, y, c: (x, y - 1, c))
Y_FAR = row_perm(lambda x, y, c: (x, y + 2, c))
X_HI = row_perm(lambda x, y, c: (x + 1, y, c))
Z_UP = col_perm(lambda z, l: (z + 1, l))
Z_DOWN = col_perm(lambda z, l: (z - 1, l))
X_LO = col_perm(lambda z, l: (z, l + 1))
FLIP = [(i * 16 + j, j * 16 + i) for i in range(16) for j in range(16)]


def send(x, axis, perm):
    return lax.ppermute(x, axis, perm)


def flip(x):
    return lax.ppermute(x, ("row", "col"), FLIP)


def cat(*xs):
    return jnp.concatenate(xs, axis=0)


def bar(*xs):
    return lax.optimization_barrier(xs)


FORWARD_OUT = (4, 4, 4, 4, 2, 2, 4, 4, 4)
BACKWARD_OUT = (4, 4, 4, 4, 16)
FORWARD_IN = ((0, 0, 16), (1, 0, 16))
BACKWARD_IN = (
    (0, 0, 4), (1, 0, 4), (2, 0, 4), (3, 0, 4), (4, 0, 2), (5, 0, 2), (6, 0, 4), (7, 0, 4), (8, 0, 4)
)


def split(x):
    high = x.astype(bf16)
    return high, (x - high.astype(f32)).astype(bf16)


def col_slot(cb, row):
    i = cb >> 1
    core = (i ^ row) & 1
    y = ((i >> 1) - (row >> 1)) & 3
    x = ((i >> 3) ^ (row >> 3)) & 1
    return (((core * 4 + y) * 2 + x) << 1) + (cb & 1)


def row_slot(rb, col):
    i = rb >> 1
    z = ((i >> 1) - (col >> 1)) & 7
    l = (i ^ col) & 1
    return ((z * 2 + l) << 1) + (rb & 1)


def product_kernel(backward, first, last, n_in, runs, out_sizes, *refs):
    rows, cols, count, here, blocks = refs[:5]
    parts, refs = refs[5 : 5 + n_in], refs[5 + n_in :]
    if not first:
        halves, total_in, refs = refs[0], refs[1], refs[2:]
    outs, refs = refs[: len(out_sizes)], refs[len(out_sizes) :]
    if first:
        halves, total, held, sems = refs
    else:
        total, held, sems = refs
    live = count[0, 0]
    bs = blocks.shape[-1]
    full = lax.div(live, UNROLL)
    middle = lax.div(full, 2)
    begin = 0 if first else middle
    end = full if last else middle

    def copy(c):
        where = pl.ds(c * UNROLL, UNROLL)
        return pltpu.make_async_copy(blocks.at[0, 0, where], held.at[where], sems.at[c])

    @pl.loop(begin, end)
    def _(c):
        copy(c).start()

    if last:

        @pl.when(full * UNROLL < live)
        def _():
            copy(full).start()

    if first:
        offset = 0
        for array, at, size in runs:

            @pl.loop(0, size)
            def _(k, part=parts[array], at=at, offset=offset):
                high, low = split(part[at + k])
                halves[offset + k, :, :bs] = high
                halves[offset + k, :, bs:] = low

            offset += size
        total[...] = jnp.zeros_like(total)
    else:
        total[...] = total_in[...]
    row, col = here[0], here[1]

    def one(s):
        rb, cb = row_slot(rows[0, 0, s], col), col_slot(cols[0, 0, s], row)
        high, low = split(held[s])
        zero = jnp.zeros_like(low)
        if backward:
            weights = jnp.concatenate(
                [jnp.concatenate([high, low], 1), jnp.concatenate([high, zero], 1)], 0
            )
            out = jnp.dot(halves[rb], weights, preferred_element_type=f32)
            total[cb] += out[:, :bs] + out[:, bs:]
        else:
            weights = jnp.concatenate(
                [jnp.concatenate([high, high], 1), jnp.concatenate([low, zero], 1)], 0
            )
            out = lax.dot_general(
                halves[cb], weights, (((1,), (1,)), ((), ())), preferred_element_type=f32
            )
            total[rb] += out[:, :bs] + out[:, bs:]

    @pl.loop(begin, end)
    def _(c):
        copy(c).wait()
        for k in range(UNROLL):
            one(c * UNROLL + k)

    if last:

        @pl.when(full * UNROLL < live)
        def _():
            copy(full).wait()

            @pl.loop(full * UNROLL, live)
            def _(s):
                one(s)

        offset = 0
        for out, size in zip(outs, out_sizes):
            out[...] = total[offset : offset + size]
            offset += size


UNROLL = 16


def products(backward, first, last, state, index):
    blocks = index[4]
    slots, bs = blocks.shape[2], blocks.shape[-1]
    vecs = state[0].shape[1]
    n_in = len(state) if first else 0
    runs = BACKWARD_IN if backward else FORWARD_IN
    out_sizes = () if not last else BACKWARD_OUT if backward else FORWARD_OUT
    smem = pl.BlockSpec(memory_space=pltpu.SMEM)
    vmem = pl.BlockSpec(memory_space=pltpu.VMEM)
    halves, total = (32, vecs, 2 * bs), (32, vecs, bs)
    out_shape = [jax.ShapeDtypeStruct((n, vecs, bs), f32) for n in out_sizes]
    scratch = []
    if first and not last:
        out_shape += [jax.ShapeDtypeStruct(halves, bf16), jax.ShapeDtypeStruct(total, f32)]
    elif first:
        scratch = [pltpu.VMEM(halves, bf16), pltpu.VMEM(total, f32)]
    else:
        scratch = [pltpu.VMEM(total, f32)]
    scratch += [
        pltpu.VMEM((slots, bs, bs), f32),
        pltpu.SemaphoreType.DMA((slots // UNROLL,)),
    ]
    share = 1 if first and last else 2
    return pl.pallas_call(
        functools.partial(product_kernel, backward, first, last, n_in, runs, out_sizes),
        in_specs=[smem] * 4 + [pl.BlockSpec(memory_space=pltpu.HBM)] + [vmem] * len(state),
        out_specs=[vmem] * len(out_shape),
        out_shape=out_shape,
        scratch_shapes=scratch,
        compiler_params=pltpu.CompilerParams(vmem_limit_bytes=48 << 20),
        cost_estimate=pl.CostEstimate(
            flops=24 * slots * vecs * bs * bs // share,
            bytes_accessed=4 * slots * bs * bs // share,
            transcendentals=0,
        ),
    )(*index, *state)


def body(vectors, blocks, block_row, block_col, block_count, lower_bound, upper_bound):
    vecs, bs = vectors.shape[0], blocks.shape[-1]
    here = jnp.stack([lax.axis_index("row"), lax.axis_index("col")]).astype(jnp.int32)
    center = (upper_bound[0] + lower_bound[0]) / 2.0
    half_width = (upper_bound[0] - lower_bound[0]) / 2.0
    index = (block_row, block_col, block_count, here, blocks)

    def apply_hamiltonian(a0, flipping, finish):
        a1 = send(a0, "row", X_HI)
        _, flipping = bar(a1, flipping)
        p0 = cat(a0, a1)
        p1 = send(p0, "row", Y_DOWN)
        p2 = send(p0, "row", Y_FAR)
        p3 = send(p0, "row", Y_UP)
        t0 = finish(flipping)
        t1 = send(t0, "col", X_LO)
        p1, p2, p3, t0, t1 = bar(p1, p2, p3, t0, t1)
        z0 = cat(t0, t1)
        up1 = send(z0, "col", Z_DOWN)
        down1 = send(z0, "col", Z_UP)
        p = cat(p0, p1, p2, p3)
        state = products(False, True, False, (p, send(p, "row", CORE)), index)
        up1, down1, *state = bar(up1, down1, *state)
        up2 = send(up1, "col", Z_DOWN)
        down2 = send(down1, "col", Z_UP)
        forward = products(False, False, True, state, index)
        up2, down2, *forward = bar(up2, down2, *forward)
        f0, f1, f2, f3, f4a, f4b, f5, f6, f7 = forward
        up3 = send(cat(up2, f4b), "col", Z_DOWN)
        down3 = send(cat(down2, f4a), "col", Z_UP)
        up3, down3 = bar(up3, down3)
        up4 = send(cat(up3[2:4], f5[:2], f5[2:] + up3[4:]), "col", Z_DOWN)
        down4 = send(cat(down3[:2], f3[:2] + down3[4:], f3[2:]), "col", Z_UP)
        up4, down4 = bar(up4, down4)
        u = send(f2 + down4[2:], "col", Z_UP)
        d = send(f6 + up4[2:], "col", Z_DOWN)
        state = (z0, up1, up2, up3, down4, up4, down3, down2, down1)
        backward = products(True, True, True, state, index)
        u, d, *backward = bar(u, d, *backward)
        g0, g1, g2, g3, other = backward
        u = send(f1 + u, "col", Z_UP)
        d = send(f7 + d, "col", Z_DOWN)
        o = send(other, "row", CORE)
        u, d, o = bar(u, d, o)
        h = send(f0[2:] + u[2:] + d[2:], "col", X_LO)
        q1 = send(g1 + o[4:8], "row", Y_UP)
        q2 = send(g2 + o[8:12], "row", Y_FAR)
        q3 = send(g3 + o[12:], "row", Y_DOWN)
        (flipped,) = bar(f0[:2] + u[:2] + d[:2] + h)
        flipped_back = flip(flipped)
        last = send(g0[2:] + o[2:4] + q1[2:] + q2[2:] + q3[2:], "row", X_HI)
        (own,) = bar(g0[:2] + o[:2] + q1[:2] + q2[:2] + q3[:2] + last)
        return own, flipped, flipped_back, t0

    y0 = vectors.reshape(vecs, -1, bs).transpose(1, 0, 2)

    def step(k, carry):
        before, now, flipping, scale, base = carry
        own, flipped, back, now_flipped = apply_hamiltonian(
            now, flip(flipping), lambda x: x * scale + base
        )
        later = (own + back - center * now) / half_width
        later = jnp.where(k == 0, later, 2.0 * later - before)
        base = (flipped - center * now_flipped) / half_width
        return now, later, own, 1.0 / half_width, base

    start = (y0, y0, y0, jnp.ones((), f32), jnp.zeros_like(y0))
    y2 = lax.fori_loop(0, 2, step, start)[1]
    return y2.transpose(1, 0, 2).reshape(vectors.shape)


def solution(mesh):
    placed = (
        P(None, ("col", "row")),
        P("row", "col", None, None, None),
        P("row", "col", None),
        P("row", "col", None),
        P("row", "col"),
        P(),
        P(),
    )
    return jax.shard_map(
        body, mesh=mesh, in_specs=placed, out_specs=P(None, ("col", "row")), check_vma=False
    )
```

```python
import functools

import jax
import jax.numpy as jnp
from jax import lax
from jax.experimental import pallas as pl
from jax.experimental.pallas import tpu as pltpu
from jax.sharding import PartitionSpec as P


f32, bf16 = jnp.float32, jnp.bfloat16

NX, NY, NC, NZ, NL = 2, 4, 2, 8, 2


def row_perm(f):
    def at(x, y, c):
        return ((x % NX) * NY + y % NY) * NC + c % NC

    return [(at(x, y, c), at(*f(x, y, c))) for x in range(NX) for y in range(NY) for c in range(NC)]


def col_perm(f):
    def at(z, l):
        return (z % NZ) * NL + l % NL

    return [(at(z, l), at(*f(z, l))) for z in range(NZ) for l in range(NL)]


CORE = row_perm(lambda x, y, c: (x, y, c + 1))
Y_UP = row_perm(lambda x, y, c: (x, y + 1, c))
Y_DOWN = row_perm(lambda x, y, c: (x, y - 1, c))
Y_FAR = row_perm(lambda x, y, c: (x, y + 2, c))
X_HI = row_perm(lambda x, y, c: (x + 1, y, c))
Z_UP = col_perm(lambda z, l: (z + 1, l))
Z_DOWN = col_perm(lambda z, l: (z - 1, l))
X_LO = col_perm(lambda z, l: (z, l + 1))
FLIP = [(i * 16 + j, j * 16 + i) for i in range(16) for j in range(16)]


def send(x, axis, perm):
    return lax.ppermute(x, axis, perm)


def flip(x):
    return lax.ppermute(x, ("row", "col"), FLIP)


def cat(*xs):
    return jnp.concatenate(xs, axis=0)


def bar(*xs):
    return lax.optimization_barrier(xs)


FORWARD_OUT = (4, 4, 4, 4, 2, 2, 4, 4, 4)
BACKWARD_OUT = (4, 4, 4, 4, 16)
FORWARD_IN = ((0, 0, 16), (1, 0, 16))
BACKWARD_IN = (
    (0, 0, 4), (1, 0, 4), (2, 0, 4), (3, 0, 4), (4, 0, 2), (5, 0, 2), (6, 0, 4), (7, 0, 4), (8, 0, 4)
)


def split(x):
    high = x.astype(bf16)
    return high, (x - high.astype(f32)).astype(bf16)


def col_slot(cb, row):
    i = cb >> 1
    core = (i ^ row) & 1
    y = ((i >> 1) - (row >> 1)) & 3
    x = ((i >> 3) ^ (row >> 3)) & 1
    return (((core * 4 + y) * 2 + x) << 1) + (cb & 1)


def row_slot(rb, col):
    i = rb >> 1
    z = ((i >> 1) - (col >> 1)) & 7
    l = (i ^ col) & 1
    return ((z * 2 + l) << 1) + (rb & 1)


def product_kernel(backward, first, last, n_in, runs, out_sizes, *refs):
    table, blocks = refs[:2]
    parts, refs = refs[2 : 2 + n_in], refs[2 + n_in :]
    if not first:
        halves, total_in, refs = refs[0], refs[1], refs[2:]
    outs, refs = refs[: len(out_sizes)], refs[len(out_sizes) :]
    if first:
        halves, total, held, sems = refs
    else:
        total, held, sems = refs
    bs, slots = blocks.shape[-1], blocks.shape[2]
    live = table[slots]
    full = lax.div(live, UNROLL)
    middle = lax.div(full, 2)
    begin = 0 if first else middle
    end = full if last else middle

    def copy(c):
        where = pl.ds(c * UNROLL, UNROLL)
        return pltpu.make_async_copy(blocks.at[0, 0, where], held.at[where], sems.at[c])

    @pl.loop(begin, end)
    def _(c):
        copy(c).start()

    if last:

        @pl.when(full * UNROLL < live)
        def _():
            copy(full).start()

    if first:
        offset = 0
        for array, at, size in runs:

            @pl.loop(0, size)
            def _(k, part=parts[array], at=at, offset=offset):
                high, low = split(part[at + k])
                halves[offset + k, :, :bs] = high
                halves[offset + k, :, bs:] = low

            offset += size
        total[...] = jnp.zeros_like(total)
    else:
        total[...] = total_in[...]

    def one(s):
        rb, cb = table[s] >> 5, table[s] & 31
        high, low = split(held[s])
        zero = jnp.zeros_like(low)
        if backward:
            weights = jnp.concatenate(
                [jnp.concatenate([high, low], 1), jnp.concatenate([high, zero], 1)], 0
            )
            out = jnp.dot(halves[rb], weights, preferred_element_type=f32)
            total[cb] += out[:, :bs] + out[:, bs:]
        else:
            weights = jnp.concatenate(
                [jnp.concatenate([high, high], 1), jnp.concatenate([low, zero], 1)], 0
            )
            out = lax.dot_general(
                halves[cb], weights, (((1,), (1,)), ((), ())), preferred_element_type=f32
            )
            total[rb] += out[:, :bs] + out[:, bs:]

    @pl.loop(begin, end)
    def _(c):
        copy(c).wait()
        for k in range(UNROLL):
            one(c * UNROLL + k)

    if last:

        @pl.when(full * UNROLL < live)
        def _():
            copy(full).wait()

            @pl.loop(full * UNROLL, live)
            def _(s):
                one(s)

        offset = 0
        for out, size in zip(outs, out_sizes):
            out[...] = total[offset : offset + size]
            offset += size


UNROLL = 16


def products(backward, first, last, state, index):
    blocks = index[1]
    slots, bs = blocks.shape[2], blocks.shape[-1]
    vecs = state[0].shape[1]
    n_in = len(state) if first else 0
    runs = BACKWARD_IN if backward else FORWARD_IN
    out_sizes = () if not last else BACKWARD_OUT if backward else FORWARD_OUT
    smem = pl.BlockSpec(memory_space=pltpu.SMEM)
    vmem = pl.BlockSpec(memory_space=pltpu.VMEM)
    halves, total = (32, vecs, 2 * bs), (32, vecs, bs)
    out_shape = [jax.ShapeDtypeStruct((n, vecs, bs), f32) for n in out_sizes]
    scratch = []
    if first and not last:
        out_shape += [jax.ShapeDtypeStruct(halves, bf16), jax.ShapeDtypeStruct(total, f32)]
    elif first:
        scratch = [pltpu.VMEM(halves, bf16), pltpu.VMEM(total, f32)]
    else:
        scratch = [pltpu.VMEM(total, f32)]
    scratch += [
        pltpu.VMEM((slots, bs, bs), f32),
        pltpu.SemaphoreType.DMA((slots // UNROLL,)),
    ]
    share = 1 if first and last else 2
    return pl.pallas_call(
        functools.partial(product_kernel, backward, first, last, n_in, runs, out_sizes),
        in_specs=[smem] + [pl.BlockSpec(memory_space=pltpu.HBM)] + [vmem] * len(state),
        out_specs=[vmem] * len(out_shape),
        out_shape=out_shape,
        scratch_shapes=scratch,
        compiler_params=pltpu.CompilerParams(vmem_limit_bytes=45 << 20),
        cost_estimate=pl.CostEstimate(
            flops=24 * slots * vecs * bs * bs // share,
            bytes_accessed=4 * slots * bs * bs // share,
            transcendentals=0,
        ),
    )(*index, *state)


def body(vectors, blocks, block_row, block_col, block_count, lower_bound, upper_bound):
    vecs, bs = vectors.shape[0], blocks.shape[-1]
    center = (upper_bound[0] + lower_bound[0]) / 2.0
    half_width = (upper_bound[0] - lower_bound[0]) / 2.0
    row, col = lax.axis_index("row"), lax.axis_index("col")
    table = row_slot(block_row[0, 0], col) * 32 + col_slot(block_col[0, 0], row)
    index = (jnp.concatenate([table, block_count[0]]), blocks)

    def apply_hamiltonian(a0, flipping, finish):
        a1 = send(a0, "row", X_HI)
        _, flipping = bar(a1, flipping)
        p0 = cat(a0, a1)
        p1 = send(p0, "row", Y_DOWN)
        p2 = send(p0, "row", Y_FAR)
        p3 = send(p0, "row", Y_UP)
        t0 = finish(flipping)
        t1 = send(t0, "col", X_LO)
        p1, p2, p3, t0, t1 = bar(p1, p2, p3, t0, t1)
        z0 = cat(t0, t1)
        up1 = send(z0, "col", Z_DOWN)
        down1 = send(z0, "col", Z_UP)
        p = cat(p0, p1, p2, p3)
        state = products(False, True, False, (p, send(p, "row", CORE)), index)
        up1, down1, *state = bar(up1, down1, *state)
        up2 = send(up1, "col", Z_DOWN)
        down2 = send(down1, "col", Z_UP)
        forward = products(False, False, True, state, index)
        up2, down2, *forward = bar(up2, down2, *forward)
        f0, f1, f2, f3, f4a, f4b, f5, f6, f7 = forward
        up3 = send(cat(up2, f4b), "col", Z_DOWN)
        down3 = send(cat(down2, f4a), "col", Z_UP)
        up3, down3 = bar(up3, down3)
        up4 = send(cat(up3[2:4], f5[:2], f5[2:] + up3[4:]), "col", Z_DOWN)
        down4 = send(cat(down3[:2], f3[:2] + down3[4:], f3[2:]), "col", Z_UP)
        up4, down4 = bar(up4, down4)
        u = send(f2 + down4[2:], "col", Z_UP)
        d = send(f6 + up4[2:], "col", Z_DOWN)
        state = (z0, up1, up2, up3, down4, up4, down3, down2, down1)
        backward = products(True, True, True, state, index)
        u, d, *backward = bar(u, d, *backward)
        g0, g1, g2, g3, other = backward
        u = send(f1 + u, "col", Z_UP)
        d = send(f7 + d, "col", Z_DOWN)
        o = send(other, "row", CORE)
        u, d, o = bar(u, d, o)
        h = send(f0[2:] + u[2:] + d[2:], "col", X_LO)
        q1 = send(g1 + o[4:8], "row", Y_UP)
        q2 = send(g2 + o[8:12], "row", Y_FAR)
        q3 = send(g3 + o[12:], "row", Y_DOWN)
        (flipped,) = bar(f0[:2] + u[:2] + d[:2] + h)
        flipped_back = flip(flipped)
        last = send(g0[2:] + o[2:4] + q1[2:] + q2[2:] + q3[2:], "row", X_HI)
        (own,) = bar(g0[:2] + o[:2] + q1[:2] + q2[:2] + q3[:2] + last)
        return own, flipped, flipped_back, t0

    y0 = vectors.reshape(vecs, -1, bs).transpose(1, 0, 2)

    def step(k, carry):
        before, now, flipping, scale, base = carry
        own, flipped, back, now_flipped = apply_hamiltonian(
            now, flip(flipping), lambda x: x * scale + base
        )
        later = (own + back - center * now) / half_width
        later = jnp.where(k == 0, later, 2.0 * later - before)
        base = (flipped - center * now_flipped) / half_width
        return now, later, own, 1.0 / half_width, base

    start = (y0, y0, y0, jnp.ones((), f32), jnp.zeros_like(y0))
    y2 = lax.fori_loop(0, 2, step, start)[1]
    return y2.transpose(1, 0, 2).reshape(vectors.shape)


def solution(mesh):
    placed = (
        P(None, ("col", "row")),
        P("row", "col", None, None, None),
        P("row", "col", None),
        P("row", "col", None),
        P("row", "col"),
        P(),
        P(),
    )
    return jax.shard_map(
        body, mesh=mesh, in_specs=placed, out_specs=P(None, ("col", "row")), check_vma=False
    )
```

```python
import functools

import jax
import jax.numpy as jnp
from jax import lax
from jax.experimental import pallas as pl
from jax.experimental.pallas import tpu as pltpu
from jax.sharding import PartitionSpec as P


f32, bf16 = jnp.float32, jnp.bfloat16

NX, NY, NC, NZ, NL = 2, 4, 2, 8, 2


def row_perm(f):
    def at(x, y, c):
        return ((x % NX) * NY + y % NY) * NC + c % NC

    return [(at(x, y, c), at(*f(x, y, c))) for x in range(NX) for y in range(NY) for c in range(NC)]


def col_perm(f):
    def at(z, l):
        return (z % NZ) * NL + l % NL

    return [(at(z, l), at(*f(z, l))) for z in range(NZ) for l in range(NL)]


CORE = row_perm(lambda x, y, c: (x, y, c + 1))
Y_UP = row_perm(lambda x, y, c: (x, y + 1, c))
Y_DOWN = row_perm(lambda x, y, c: (x, y - 1, c))
Y_FAR = row_perm(lambda x, y, c: (x, y + 2, c))
X_HI = row_perm(lambda x, y, c: (x + 1, y, c))
Z_UP = col_perm(lambda z, l: (z + 1, l))
Z_DOWN = col_perm(lambda z, l: (z - 1, l))
X_LO = col_perm(lambda z, l: (z, l + 1))
FLIP = [(i * 16 + j, j * 16 + i) for i in range(16) for j in range(16)]


def send(x, axis, perm):
    return lax.ppermute(x, axis, perm)


def flip(x):
    return lax.ppermute(x, ("row", "col"), FLIP)


def cat(*xs):
    return jnp.concatenate(xs, axis=0)


def bar(*xs):
    return lax.optimization_barrier(xs)


FORWARD_OUT = (4, 4, 4, 4, 2, 2, 4, 4, 4)
BACKWARD_OUT = (4, 4, 4, 4, 16)
FORWARD_IN = ((0, 0, 16), (1, 0, 16))
BACKWARD_IN = (
    (0, 0, 4), (1, 0, 4), (2, 0, 4), (3, 0, 4), (4, 0, 2), (5, 0, 2), (6, 0, 4), (7, 0, 4), (8, 0, 4)
)


def split(x):
    high = x.astype(bf16)
    return high, (x - high.astype(f32)).astype(bf16)


def col_slot(cb, row):
    i = cb >> 1
    core = (i ^ row) & 1
    y = ((i >> 1) - (row >> 1)) & 3
    x = ((i >> 3) ^ (row >> 3)) & 1
    return (((core * 4 + y) * 2 + x) << 1) + (cb & 1)


def row_slot(rb, col):
    i = rb >> 1
    z = ((i >> 1) - (col >> 1)) & 7
    l = (i ^ col) & 1
    return ((z * 2 + l) << 1) + (rb & 1)


def product_kernel(backward, first, last, n_in, runs, out_sizes, *refs):
    rows, cols, info, blocks = refs[:4]
    parts, refs = refs[4 : 4 + n_in], refs[4 + n_in :]
    if not first:
        halves, total_in, refs = refs[0], refs[1], refs[2:]
    outs, refs = refs[: len(out_sizes)], refs[len(out_sizes) :]
    if first:
        halves, total, held, sems = refs
    else:
        total, held, sems = refs
    bs = blocks.shape[-1]
    row, col, live = info[0], info[1], info[2]
    full = lax.div(live, UNROLL)
    middle = lax.div(full, 2)
    begin = 0 if first else middle
    end = full if last else middle

    def copy(c):
        where = pl.ds(c * UNROLL, UNROLL)
        return pltpu.make_async_copy(blocks.at[0, 0, where], held.at[where], sems.at[c])

    @pl.loop(begin, end)
    def _(c):
        copy(c).start()

    if last:

        @pl.when(full * UNROLL < live)
        def _():
            copy(full).start()

    if first:
        offset = 0
        for array, at, size in runs:

            @pl.loop(0, size)
            def _(k, part=parts[array], at=at, offset=offset):
                high, low = split(part[at + k])
                halves[offset + k, :, :bs] = high
                halves[offset + k, :, bs:] = low

            offset += size
        total[...] = jnp.zeros_like(total)
    else:
        total[...] = total_in[...]

    def one(s):
        rb, cb = row_slot(rows[0, 0, s], col), col_slot(cols[0, 0, s], row)
        high, low = split(held[s])
        zero = jnp.zeros_like(low)
        if backward:
            weights = jnp.concatenate(
                [jnp.concatenate([high, low], 1), jnp.concatenate([high, zero], 1)], 0
            )
            out = jnp.dot(halves[rb], weights, preferred_element_type=f32)
            total[cb] += out[:, :bs] + out[:, bs:]
        else:
            weights = jnp.concatenate(
                [jnp.concatenate([high, high], 1), jnp.concatenate([low, zero], 1)], 0
            )
            out = lax.dot_general(
                halves[cb], weights, (((1,), (1,)), ((), ())), preferred_element_type=f32
            )
            total[rb] += out[:, :bs] + out[:, bs:]

    @pl.loop(begin, end)
    def _(c):
        copy(c).wait()
        for k in range(UNROLL):
            one(c * UNROLL + k)

    if last:

        @pl.when(full * UNROLL < live)
        def _():
            copy(full).wait()

            @pl.loop(full * UNROLL, live)
            def _(s):
                one(s)

        offset = 0
        for out, size in zip(outs, out_sizes):
            out[...] = total[offset : offset + size]
            offset += size


UNROLL = 16


def products(backward, first, last, state, index):
    blocks = index[3]
    slots, bs = blocks.shape[2], blocks.shape[-1]
    vecs = state[0].shape[1]
    n_in = len(state) if first else 0
    runs = BACKWARD_IN if backward else FORWARD_IN
    out_sizes = () if not last else BACKWARD_OUT if backward else FORWARD_OUT
    smem = pl.BlockSpec(memory_space=pltpu.SMEM)
    vmem = pl.BlockSpec(memory_space=pltpu.VMEM)
    halves, total = (32, vecs, 2 * bs), (32, vecs, bs)
    out_shape = [jax.ShapeDtypeStruct((n, vecs, bs), f32) for n in out_sizes]
    scratch = []
    if first and not last:
        out_shape += [jax.ShapeDtypeStruct(halves, bf16), jax.ShapeDtypeStruct(total, f32)]
    elif first:
        scratch = [pltpu.VMEM(halves, bf16), pltpu.VMEM(total, f32)]
    else:
        scratch = [pltpu.VMEM(total, f32)]
    scratch += [
        pltpu.VMEM((slots, bs, bs), f32),
        pltpu.SemaphoreType.DMA((slots // UNROLL,)),
    ]
    share = 1 if first and last else 2
    return pl.pallas_call(
        functools.partial(product_kernel, backward, first, last, n_in, runs, out_sizes),
        in_specs=[smem] * 3 + [pl.BlockSpec(memory_space=pltpu.HBM)] + [vmem] * len(state),
        out_specs=[vmem] * len(out_shape),
        out_shape=out_shape,
        scratch_shapes=scratch,
        compiler_params=pltpu.CompilerParams(vmem_limit_bytes=49 << 20),
        cost_estimate=pl.CostEstimate(
            flops=24 * slots * vecs * bs * bs // share,
            bytes_accessed=4 * slots * bs * bs // share,
            transcendentals=0,
        ),
    )(*index, *state)


def body(vectors, blocks, block_row, block_col, block_count, lower_bound, upper_bound):
    vecs, bs = vectors.shape[0], blocks.shape[-1]
    center = (upper_bound[0] + lower_bound[0]) / 2.0
    half_width = (upper_bound[0] - lower_bound[0]) / 2.0
    here = (lax.axis_index("row"), lax.axis_index("col"), block_count[0, 0])
    index = (block_row, block_col, jnp.stack(here).astype(jnp.int32), blocks)

    def apply_hamiltonian(a0, flipping, finish):
        a1 = send(a0, "row", X_HI)
        _, flipping = bar(a1, flipping)
        p0 = cat(a0, a1)
        p1 = send(p0, "row", Y_DOWN)
        p2 = send(p0, "row", Y_FAR)
        p3 = send(p0, "row", Y_UP)
        t0 = finish(flipping)
        t1 = send(t0, "col", X_LO)
        p1, p2, p3, t0, t1 = bar(p1, p2, p3, t0, t1)
        z0 = cat(t0, t1)
        up1 = send(z0, "col", Z_DOWN)
        down1 = send(z0, "col", Z_UP)
        p = cat(p0, p1, p2, p3)
        state = products(False, True, False, (p, send(p, "row", CORE)), index)
        up1, down1, *state = bar(up1, down1, *state)
        up2 = send(up1, "col", Z_DOWN)
        down2 = send(down1, "col", Z_UP)
        forward = products(False, False, True, state, index)
        up2, down2, *forward = bar(up2, down2, *forward)
        f0, f1, f2, f3, f4a, f4b, f5, f6, f7 = forward
        up3 = send(cat(up2, f4b), "col", Z_DOWN)
        down3 = send(cat(down2, f4a), "col", Z_UP)
        up3, down3 = bar(up3, down3)
        up4 = send(cat(up3[2:4], f5[:2], f5[2:] + up3[4:]), "col", Z_DOWN)
        down4 = send(cat(down3[:2], f3[:2] + down3[4:], f3[2:]), "col", Z_UP)
        up4, down4 = bar(up4, down4)
        u = send(f2 + down4[2:], "col", Z_UP)
        d = send(f6 + up4[2:], "col", Z_DOWN)
        u, d = bar(u, d)
        u = send(f1 + u, "col", Z_UP)
        d = send(f7 + d, "col", Z_DOWN)
        state = (z0, up1, up2, up3, down4, up4, down3, down2, down1)
        backward = products(True, True, True, state, index)
        u, d, *backward = bar(u, d, *backward)
        g0, g1, g2, g3, other = backward
        h = send(f0[2:] + u[2:] + d[2:], "col", X_LO)
        o = send(other, "row", CORE)
        q1 = send(g1 + o[4:8], "row", Y_UP)
        q2 = send(g2 + o[8:12], "row", Y_FAR)
        q3 = send(g3 + o[12:], "row", Y_DOWN)
        (flipped,) = bar(f0[:2] + u[:2] + d[:2] + h)
        flipped_back = flip(flipped)
        last = send(g0[2:] + o[2:4] + q1[2:] + q2[2:] + q3[2:], "row", X_HI)
        (own,) = bar(g0[:2] + o[:2] + q1[:2] + q2[:2] + q3[:2] + last)
        return own, flipped, flipped_back, t0

    y0 = vectors.reshape(vecs, -1, bs).transpose(1, 0, 2)

    def step(k, carry):
        before, now, flipping, scale, base = carry
        own, flipped, back, now_flipped = apply_hamiltonian(
            now, flip(flipping), lambda x: x * scale + base
        )
        later = (own + back - center * now) / half_width
        later = jnp.where(k == 0, later, 2.0 * later - before)
        base = (flipped - center * now_flipped) / half_width
        return now, later, own, 1.0 / half_width, base

    start = (y0, y0, y0, jnp.ones((), f32), jnp.zeros_like(y0))
    y2 = lax.fori_loop(0, 2, step, start)[1]
    return y2.transpose(1, 0, 2).reshape(vectors.shape)


def solution(mesh):
    placed = (
        P(None, ("col", "row")),
        P("row", "col", None, None, None),
        P("row", "col", None),
        P("row", "col", None),
        P("row", "col"),
        P(),
        P(),
    )
    return jax.shard_map(
        body, mesh=mesh, in_specs=placed, out_specs=P(None, ("col", "row")), check_vma=False
    )
```

```python
import functools

import jax
import jax.numpy as jnp
from jax import lax
from jax.experimental import pallas as pl
from jax.experimental.pallas import tpu as pltpu
from jax.sharding import PartitionSpec as P


f32, bf16 = jnp.float32, jnp.bfloat16

NX, NY, NC, NZ, NL = 2, 4, 2, 8, 2


def row_perm(f):
    def at(x, y, c):
        return ((x % NX) * NY + y % NY) * NC + c % NC

    return [(at(x, y, c), at(*f(x, y, c))) for x in range(NX) for y in range(NY) for c in range(NC)]


def col_perm(f):
    def at(z, l):
        return (z % NZ) * NL + l % NL

    return [(at(z, l), at(*f(z, l))) for z in range(NZ) for l in range(NL)]


CORE = row_perm(lambda x, y, c: (x, y, c + 1))
Y_UP = row_perm(lambda x, y, c: (x, y + 1, c))
Y_DOWN = row_perm(lambda x, y, c: (x, y - 1, c))
Y_FAR = row_perm(lambda x, y, c: (x, y + 2, c))
X_HI = row_perm(lambda x, y, c: (x + 1, y, c))
Z_UP = col_perm(lambda z, l: (z + 1, l))
Z_DOWN = col_perm(lambda z, l: (z - 1, l))
X_LO = col_perm(lambda z, l: (z, l + 1))
FLIP = [(i * 16 + j, j * 16 + i) for i in range(16) for j in range(16)]


def send(x, axis, perm):
    return lax.ppermute(x, axis, perm)


def flip(x):
    return lax.ppermute(x, ("row", "col"), FLIP)


def cat(*xs):
    return jnp.concatenate(xs, axis=0)


def bar(*xs):
    return lax.optimization_barrier(xs)


FORWARD_OUT = (4, 4, 4, 4, 2, 2, 4, 4, 4)
BACKWARD_OUT = (4, 4, 4, 4, 16)
FORWARD_IN = ((0, 0, 0, 16), (1, 0, 16, 16))
BACKWARD_IN = tuple((k, 0, at, 4) for k, at in enumerate((0, 4, 8, 12, 20, 24, 28)))
FAR = 16


def split(x):
    high = x.astype(bf16)
    return high, (x - high.astype(f32)).astype(bf16)


def col_slot(cb, row):
    i = cb >> 1
    core = (i ^ row) & 1
    y = ((i >> 1) - (row >> 1)) & 3
    x = ((i >> 3) ^ (row >> 3)) & 1
    return (((core * 4 + y) * 2 + x) << 1) + (cb & 1)


def row_slot(rb, col):
    i = rb >> 1
    z = ((i >> 1) - (col >> 1)) & 7
    l = (i ^ col) & 1
    return ((z * 2 + l) << 1) + (rb & 1)


def spread_halves(parts, runs, halves):
    bs = halves.shape[-1] // 2
    for array, at, slot, size in runs:

        @pl.loop(0, size)
        def _(k, part=parts[array], at=at, slot=slot):
            high, low = split(part[at + k])
            halves[slot + k, :, :bs] = high
            halves[slot + k, :, bs:] = low


def product(source, block, backward):
    bs = block.shape[-1]
    high, low = split(block)
    zero = jnp.zeros_like(low)
    side, down = (1, 0) if backward else (0, 1)
    first = jnp.concatenate([high, low], side)
    weights = jnp.concatenate([first, jnp.concatenate([high, zero], side)], down)
    contract = (((1,), (0 if backward else 1,)), ((), ()))
    out = lax.dot_general(source, weights, contract, preferred_element_type=f32)
    return out[:, :bs] + out[:, bs:]


def write_out(total, outs, sizes):
    offset = 0
    for out, size in zip(outs, sizes):
        out[...] = total[offset : offset + size]
        offset += size


def product_kernel(backward, first, last, n_in, runs, out_sizes, *refs):
    rows, cols, info, blocks = refs[:4]
    parts, refs = refs[4 : 4 + n_in], refs[4 + n_in :]
    if not first:
        halves, total_in, refs = refs[0], refs[1], refs[2:]
    outs, refs = refs[: len(out_sizes)], refs[len(out_sizes) :]
    if backward:
        total, halves, held, sems = refs
    elif first:
        halves, total, held, sems = refs
    else:
        total, held, sems = refs
    row, col, live = info[0], info[1], info[2]
    full = lax.div(live, UNROLL)
    middle = lax.div(full, 2)
    begin = 0 if first else middle
    end = full if last else middle

    def copy(c):
        where = pl.ds(c * UNROLL, UNROLL)
        return pltpu.make_async_copy(blocks.at[0, 0, where], held.at[where], sems.at[c])

    @pl.loop(begin, end)
    def _(c):
        copy(c).start()

    if last:

        @pl.when(full * UNROLL < live)
        def _():
            copy(full).start()

    if first:
        spread_halves(parts, runs, halves)
        total[...] = jnp.zeros_like(total)
        if backward:
            halves[FAR : FAR + 4] = jnp.zeros((4,) + halves.shape[1:], bf16)
    else:
        total[...] = total_in[...]

    def one(s):
        rb, cb = row_slot(rows[0, 0, s], col), col_slot(cols[0, 0, s], row)
        source, target = (rb, cb) if backward else (cb, rb)
        total[target] += product(halves[source], held[s], backward)

    @pl.loop(begin, end)
    def _(c):
        copy(c).wait()
        for k in range(UNROLL):
            one(c * UNROLL + k)

    if last:

        @pl.when(full * UNROLL < live)
        def _():
            copy(full).wait()

            @pl.loop(full * UNROLL, live)
            def _(s):
                one(s)

        write_out(total, outs, out_sizes)


def far_kernel(runs, out_sizes, *refs):
    rows, cols, info, blocks, far_a, far_b, total_in = refs[:7]
    outs, (halves, total, held, picked, sems) = refs[7:-5], refs[-5:]
    row, col, live = info[0], info[1], info[2]

    def copy(s, n):
        return pltpu.make_async_copy(blocks.at[0, 0, s], held.at[n], sems.at[n])

    def pick(s, n):
        far = row_slot(rows[0, 0, s], col) >> 2 == FAR >> 2

        @pl.when(far)
        def _():
            picked[n] = s
            copy(s, n).start()

        return n + far.astype(jnp.int32)

    found = lax.fori_loop(0, live, pick, jnp.int32(0))
    spread_halves((far_a, far_b), runs, halves)
    spare = total_in.shape[0]
    total[:spare] = total_in[...]
    total[spare] = jnp.zeros(total.shape[1:], f32)

    @pl.loop(0, lax.div(found + FAR_UNROLL - 1, FAR_UNROLL))
    def _(g):
        for k in range(FAR_UNROLL):
            n = g * FAR_UNROLL + k

            @pl.when(n < found)
            def _(n=n):
                copy(picked[n], n).wait()

        for k in range(FAR_UNROLL):
            n = g * FAR_UNROLL + k
            at = jnp.minimum(n, found - 1)
            s = picked[at]
            rb, cb = row_slot(rows[0, 0, s], col), col_slot(cols[0, 0, s], row)
            cb = jnp.where(n < found, cb, spare)
            total[cb] += product(halves[rb & 3], held[at], True)

    write_out(total, outs, out_sizes)


FAR_UNROLL = 4
UNROLL = 16


def products(backward, first, last, state, index):
    blocks = index[3]
    slots, bs = blocks.shape[2], blocks.shape[-1]
    vecs = state[0].shape[1]
    far = backward and not first
    out_sizes = () if not last else BACKWARD_OUT if backward else FORWARD_OUT
    smem = pl.BlockSpec(memory_space=pltpu.SMEM)
    vmem = pl.BlockSpec(memory_space=pltpu.VMEM)
    halves, total = (32, vecs, 2 * bs), (32, vecs, bs)
    out_shape = [jax.ShapeDtypeStruct((n, vecs, bs), f32) for n in out_sizes]
    scratch = []
    held = [pltpu.VMEM((slots, bs, bs), f32), pltpu.SemaphoreType.DMA((slots // UNROLL,))]
    if far:
        kernel = functools.partial(far_kernel, ((0, 0, 0, 2), (1, 0, 2, 2)), out_sizes)
        scratch = [pltpu.VMEM((4,) + halves[1:], bf16), pltpu.VMEM((33,) + total[1:], f32), held[0]]
        held = [pltpu.SMEM((slots,), jnp.int32), pltpu.SemaphoreType.DMA((slots,))]
    else:
        n_in = len(state) if first else 0
        runs = BACKWARD_IN if backward else FORWARD_IN
        kernel = functools.partial(
            product_kernel, backward, first, last or backward, n_in, runs, out_sizes
        )
        if backward:
            out_shape += [jax.ShapeDtypeStruct(total, f32)]
            scratch = [pltpu.VMEM(halves, bf16)]
        elif first:
            out_shape += [jax.ShapeDtypeStruct(halves, bf16), jax.ShapeDtypeStruct(total, f32)]
        else:
            scratch = [pltpu.VMEM(total, f32)]
    share = 8 if far else 1 if backward else 2
    return pl.pallas_call(
        kernel,
        in_specs=[smem] * 3 + [pl.BlockSpec(memory_space=pltpu.HBM)] + [vmem] * len(state),
        out_specs=[vmem] * len(out_shape),
        out_shape=out_shape,
        scratch_shapes=scratch + held,
        compiler_params=pltpu.CompilerParams(vmem_limit_bytes=49 << 20),
        cost_estimate=pl.CostEstimate(
            flops=24 * slots * vecs * bs * bs // share,
            bytes_accessed=4 * slots * bs * bs // share,
            transcendentals=0,
        ),
    )(*index, *state)


def body(vectors, blocks, block_row, block_col, block_count, lower_bound, upper_bound):
    vecs, bs = vectors.shape[0], blocks.shape[-1]
    center = (upper_bound[0] + lower_bound[0]) / 2.0
    half_width = (upper_bound[0] - lower_bound[0]) / 2.0
    here = (lax.axis_index("row"), lax.axis_index("col"), block_count[0, 0])
    index = (block_row, block_col, jnp.stack(here).astype(jnp.int32), blocks)

    def apply_hamiltonian(a0, flipping, finish):
        a1 = send(a0, "row", X_HI)
        _, flipping = bar(a1, flipping)
        p0 = cat(a0, a1)
        p1 = send(p0, "row", Y_DOWN)
        p2 = send(p0, "row", Y_FAR)
        p3 = send(p0, "row", Y_UP)
        t0 = finish(flipping)
        t1 = send(t0, "col", X_LO)
        p1, p2, p3, t0, t1 = bar(p1, p2, p3, t0, t1)
        z0 = cat(t0, t1)
        up1 = send(z0, "col", Z_DOWN)
        down1 = send(z0, "col", Z_UP)
        p = cat(p0, p1, p2, p3)
        state = products(False, True, False, (p, send(p, "row", CORE)), index)
        up1, down1, *state = bar(up1, down1, *state)
        up2 = send(up1, "col", Z_DOWN)
        down2 = send(down1, "col", Z_UP)
        forward = products(False, False, True, state, index)
        up2, down2, *forward = bar(up2, down2, *forward)
        f0, f1, f2, f3, f4a, f4b, f5, f6, f7 = forward
        up3 = send(cat(up2, f4b), "col", Z_DOWN)
        down3 = send(cat(down2, f4a), "col", Z_UP)
        up3, down3 = bar(up3, down3)
        up4 = send(cat(up3[2:4], f5[:2], f5[2:] + up3[4:]), "col", Z_DOWN)
        down4 = send(cat(down3[:2], f3[:2] + down3[4:], f3[2:]), "col", Z_UP)
        state = (z0, up1, up2, up3, down3, down2, down1)
        (total,) = products(True, True, False, state, index)
        up4, down4, total = bar(up4, down4, total)
        u = send(f2 + down4[2:], "col", Z_UP)
        d = send(f6 + up4[2:], "col", Z_DOWN)
        backward = products(True, False, True, (down4, up4, total), index)
        u, d, *backward = bar(u, d, *backward)
        g0, g1, g2, g3, other = backward
        u = send(f1 + u, "col", Z_UP)
        d = send(f7 + d, "col", Z_DOWN)
        o = send(other, "row", CORE)
        u, d, o = bar(u, d, o)
        h = send(f0[2:] + u[2:] + d[2:], "col", X_LO)
        q1 = send(g1 + o[4:8], "row", Y_UP)
        q2 = send(g2 + o[8:12], "row", Y_FAR)
        q3 = send(g3 + o[12:], "row", Y_DOWN)
        (flipped,) = bar(f0[:2] + u[:2] + d[:2] + h)
        flipped_back = flip(flipped)
        last = send(g0[2:] + o[2:4] + q1[2:] + q2[2:] + q3[2:], "row", X_HI)
        (own,) = bar(g0[:2] + o[:2] + q1[:2] + q2[:2] + q3[:2] + last)
        return own, flipped, flipped_back, t0

    y0 = vectors.reshape(vecs, -1, bs).transpose(1, 0, 2)

    def step(k, carry):
        before, now, flipping, scale, base = carry
        own, flipped, back, now_flipped = apply_hamiltonian(
            now, flip(flipping), lambda x: x * scale + base
        )
        later = (own + back - center * now) / half_width
        later = jnp.where(k == 0, later, 2.0 * later - before)
        base = (flipped - center * now_flipped) / half_width
        return now, later, own, 1.0 / half_width, base

    start = (y0, y0, y0, jnp.ones((), f32), jnp.zeros_like(y0))
    y2 = lax.fori_loop(0, 2, step, start)[1]
    return y2.transpose(1, 0, 2).reshape(vectors.shape)


def solution(mesh):
    placed = (
        P(None, ("col", "row")),
        P("row", "col", None, None, None),
        P("row", "col", None),
        P("row", "col", None),
        P("row", "col"),
        P(),
        P(),
    )
    return jax.shard_map(
        body, mesh=mesh, in_specs=placed, out_specs=P(None, ("col", "row")), check_vma=False
    )
```

```python
import functools

import jax
import jax.numpy as jnp
from jax import lax
from jax.experimental import pallas as pl
from jax.experimental.pallas import tpu as pltpu
from jax.sharding import PartitionSpec as P


f32, bf16 = jnp.float32, jnp.bfloat16

NX, NY, NC, NZ, NL = 2, 4, 2, 8, 2


def row_perm(f):
    def at(x, y, c):
        return ((x % NX) * NY + y % NY) * NC + c % NC

    return [(at(x, y, c), at(*f(x, y, c))) for x in range(NX) for y in range(NY) for c in range(NC)]


def col_perm(f):
    def at(z, l):
        return (z % NZ) * NL + l % NL

    return [(at(z, l), at(*f(z, l))) for z in range(NZ) for l in range(NL)]


CORE = row_perm(lambda x, y, c: (x, y, c + 1))
Y_UP = row_perm(lambda x, y, c: (x, y + 1, c))
Y_DOWN = row_perm(lambda x, y, c: (x, y - 1, c))
Y_FAR = row_perm(lambda x, y, c: (x, y + 2, c))
X_HI = row_perm(lambda x, y, c: (x + 1, y, c))
Z_UP = col_perm(lambda z, l: (z + 1, l))
Z_DOWN = col_perm(lambda z, l: (z - 1, l))
X_LO = col_perm(lambda z, l: (z, l + 1))
FLIP = [(i * 16 + j, j * 16 + i) for i in range(16) for j in range(16)]


def send(x, axis, perm):
    return lax.ppermute(x, axis, perm)


def flip(x):
    return lax.ppermute(x, ("row", "col"), FLIP)


def cat(*xs):
    return jnp.concatenate(xs, axis=0)


def bar(*xs):
    return lax.optimization_barrier(xs)


FORWARD_OUT = (4, 4, 4, 4, 2, 2, 4, 4, 4)
BACKWARD_OUT = (4, 4, 4, 4, 16)
FORWARD_IN = ((0, 0, 0, 16), (1, 0, 16, 16))
BACKWARD_IN = tuple((k, 0, at, 4) for k, at in enumerate((0, 4, 8, 12, 20, 24, 28)))
FAR = 16


def split(x):
    high = x.astype(bf16)
    return high, (x - high.astype(f32)).astype(bf16)


def col_slot(cb, row):
    i = cb >> 1
    core = (i ^ row) & 1
    y = ((i >> 1) - (row >> 1)) & 3
    x = ((i >> 3) ^ (row >> 3)) & 1
    return (((core * 4 + y) * 2 + x) << 1) + (cb & 1)


def row_slot(rb, col):
    i = rb >> 1
    z = ((i >> 1) - (col >> 1)) & 7
    l = (i ^ col) & 1
    return ((z * 2 + l) << 1) + (rb & 1)


def spread_halves(parts, runs, halves):
    bs = halves.shape[-1] // 2
    for array, at, slot, size in runs:

        @pl.loop(0, size)
        def _(k, part=parts[array], at=at, slot=slot):
            high, low = split(part[at + k])
            halves[slot + k, :, :bs] = high
            halves[slot + k, :, bs:] = low


def product(source, block, backward):
    bs = block.shape[-1]
    high, low = split(block)
    zero = jnp.zeros_like(low)
    side, down = (1, 0) if backward else (0, 1)
    first = jnp.concatenate([high, low], side)
    weights = jnp.concatenate([first, jnp.concatenate([high, zero], side)], down)
    contract = (((1,), (0 if backward else 1,)), ((), ()))
    out = lax.dot_general(source, weights, contract, preferred_element_type=f32)
    return out[:, :bs] + out[:, bs:]


def write_out(total, outs, sizes):
    offset = 0
    for out, size in zip(outs, sizes):
        out[...] = total[offset : offset + size]
        offset += size


def product_kernel(backward, first, last, n_in, runs, out_sizes, *refs):
    rows, cols, info, blocks = refs[:4]
    parts, refs = refs[4 : 4 + n_in], refs[4 + n_in :]
    if not first:
        halves, total_in, refs = refs[0], refs[1], refs[2:]
    outs, refs = refs[: len(out_sizes)], refs[len(out_sizes) :]
    if backward:
        total, halves, held, sems = refs
    elif first:
        halves, total, held, sems = refs
    else:
        total, held, sems = refs
    row, col, live = info[0], info[1], info[2]
    full = lax.div(live, UNROLL)
    middle = lax.div(full, 2)
    begin = 0 if first else middle
    end = full if last else middle

    def copy(c):
        where = pl.ds(c * UNROLL, UNROLL)
        return pltpu.make_async_copy(blocks.at[0, 0, where], held.at[where], sems.at[c])

    @pl.loop(begin, end)
    def _(c):
        copy(c).start()

    if last:

        @pl.when(full * UNROLL < live)
        def _():
            copy(full).start()

    if first:
        spread_halves(parts, runs, halves)
        total[...] = jnp.zeros_like(total)
        if backward:
            halves[FAR : FAR + 4] = jnp.zeros((4,) + halves.shape[1:], bf16)
    else:
        total[...] = total_in[...]

    def one(s):
        rb, cb = row_slot(rows[0, 0, s], col), col_slot(cols[0, 0, s], row)
        source, target = (rb, cb) if backward else (cb, rb)
        total[target] += product(halves[source], held[s], backward)

    @pl.loop(begin, end)
    def _(c):
        copy(c).wait()
        for k in range(UNROLL):
            one(c * UNROLL + k)

    if last:

        @pl.when(full * UNROLL < live)
        def _():
            copy(full).wait()

            @pl.loop(full * UNROLL, live)
            def _(s):
                one(s)

        write_out(total, outs, out_sizes)


def far_kernel(runs, out_sizes, *refs):
    rows, cols, info, blocks, far_a, far_b, total_in = refs[:7]
    outs, (halves, total, held, picked, sems) = refs[7:-5], refs[-5:]
    row, col, live = info[0], info[1], info[2]

    def copy(s, n):
        return pltpu.make_async_copy(blocks.at[0, 0, s], held.at[n], sems.at[n])

    def pick(s, n):
        far = row_slot(rows[0, 0, s], col) >> 2 == FAR >> 2

        @pl.when(far)
        def _():
            picked[n] = s
            copy(s, n).start()

        return n + far.astype(jnp.int32)

    found = lax.fori_loop(0, live, pick, jnp.int32(0))
    spread_halves((far_a, far_b), runs, halves)
    spare = total_in.shape[0]
    total[:spare] = total_in[...]
    total[spare] = jnp.zeros(total.shape[1:], f32)

    @pl.loop(0, lax.div(found + FAR_UNROLL - 1, FAR_UNROLL))
    def _(g):
        for k in range(FAR_UNROLL):
            n = g * FAR_UNROLL + k

            @pl.when(n < found)
            def _(n=n):
                copy(picked[n], n).wait()

        for k in range(FAR_UNROLL):
            n = g * FAR_UNROLL + k
            at = jnp.minimum(n, found - 1)
            s = picked[at]
            rb, cb = row_slot(rows[0, 0, s], col), col_slot(cols[0, 0, s], row)
            cb = jnp.where(n < found, cb, spare)
            total[cb] += product(halves[rb & 3], held[at], True)

    write_out(total, outs, out_sizes)


FAR_UNROLL = 4
UNROLL = 16


def products(backward, first, last, state, index):
    blocks = index[3]
    slots, bs = blocks.shape[2], blocks.shape[-1]
    vecs = state[0].shape[1]
    far = backward and not first
    out_sizes = () if not last else BACKWARD_OUT if backward else FORWARD_OUT
    smem = pl.BlockSpec(memory_space=pltpu.SMEM)
    vmem = pl.BlockSpec(memory_space=pltpu.VMEM)
    halves, total = (32, vecs, 2 * bs), (32, vecs, bs)
    out_shape = [jax.ShapeDtypeStruct((n, vecs, bs), f32) for n in out_sizes]
    scratch = []
    held = [pltpu.VMEM((slots, bs, bs), f32), pltpu.SemaphoreType.DMA((slots // UNROLL,))]
    if far:
        kernel = functools.partial(far_kernel, ((0, 0, 0, 2), (1, 0, 2, 2)), out_sizes)
        scratch = [pltpu.VMEM((4,) + halves[1:], bf16), pltpu.VMEM((33,) + total[1:], f32), held[0]]
        held = [pltpu.SMEM((slots,), jnp.int32), pltpu.SemaphoreType.DMA((slots,))]
    else:
        n_in = len(state) if first else 0
        runs = BACKWARD_IN if backward else FORWARD_IN
        kernel = functools.partial(
            product_kernel, backward, first, last or backward, n_in, runs, out_sizes
        )
        if backward:
            out_shape += [jax.ShapeDtypeStruct(total, f32)]
            scratch = [pltpu.VMEM(halves, bf16)]
        elif first:
            out_shape += [jax.ShapeDtypeStruct(halves, bf16), jax.ShapeDtypeStruct(total, f32)]
        else:
            scratch = [pltpu.VMEM(total, f32)]
    share = 8 if far else 1 if backward else 2
    return pl.pallas_call(
        kernel,
        in_specs=[smem] * 3 + [pl.BlockSpec(memory_space=pltpu.HBM)] + [vmem] * len(state),
        out_specs=[vmem] * len(out_shape),
        out_shape=out_shape,
        scratch_shapes=scratch + held,
        compiler_params=pltpu.CompilerParams(vmem_limit_bytes=24 << 20),
        cost_estimate=pl.CostEstimate(
            flops=24 * slots * vecs * bs * bs // share,
            bytes_accessed=4 * slots * bs * bs // share,
            transcendentals=0,
        ),
    )(*index, *state)


def body(vectors, blocks, block_row, block_col, block_count, lower_bound, upper_bound):
    vecs, bs = vectors.shape[0], blocks.shape[-1]
    center = (upper_bound[0] + lower_bound[0]) / 2.0
    half_width = (upper_bound[0] - lower_bound[0]) / 2.0
    here = (lax.axis_index("row"), lax.axis_index("col"), block_count[0, 0])
    index = (block_row, block_col, jnp.stack(here).astype(jnp.int32), pltpu.with_memory_space_constraint(blocks, pltpu.HBM))

    def apply_hamiltonian(a0, flipping, offset, finish):
        a1 = send(a0, "row", X_HI)
        _, flipping, offset = bar(a1, flipping, offset)
        p0 = cat(a0, a1)
        p1 = send(p0, "row", Y_DOWN)
        p2 = send(p0, "row", Y_FAR)
        p3 = send(p0, "row", Y_UP)
        t0 = finish(flipping, offset)
        t1 = send(t0, "col", X_LO)
        p1, p2, p3, t0, t1 = bar(p1, p2, p3, t0, t1)
        z0 = cat(t0, t1)
        up1 = send(z0, "col", Z_DOWN)
        down1 = send(z0, "col", Z_UP)
        p = cat(p0, p1, p2, p3)
        c = send(p, "row", CORE)
        state = products(False, True, False, (p, c), index)
        up1, down1, *state = bar(up1, down1, *state)
        up2 = send(up1, "col", Z_DOWN)
        down2 = send(down1, "col", Z_UP)
        forward = products(False, False, True, state, index)
        up2, down2, *forward = bar(up2, down2, *forward)
        f0, f1, f2, f3, f4a, f4b, f5, f6, f7 = forward
        up3 = send(cat(up2, f4b), "col", Z_DOWN)
        down3 = send(cat(down2, f4a), "col", Z_UP)
        up3, down3 = bar(up3, down3)
        up4 = send(cat(up3[2:4], f5[:2], f5[2:] + up3[4:]), "col", Z_DOWN)
        down4 = send(cat(down3[:2], f3[:2] + down3[4:], f3[2:]), "col", Z_UP)
        state = (z0, up1, up2, up3, down3, down2, down1)
        (total,) = products(True, True, False, state, index)
        up4, down4, total = bar(up4, down4, total)
        u = send(f2 + down4[2:], "col", Z_UP)
        d = send(f6 + up4[2:], "col", Z_DOWN)
        backward = products(True, False, True, (down4, up4, total), index)
        u, d, *backward = bar(u, d, *backward)
        g0, g1, g2, g3, other = backward
        u = send(f1 + u, "col", Z_UP)
        d = send(f7 + d, "col", Z_DOWN)
        o = send(other, "row", CORE)
        keep, away = bar(f0[:2] + u[:2] + d[:2], f0[2:] + u[2:] + d[2:])
        h = send(away, "col", X_LO)
        q1 = send(g1 + o[4:8], "row", Y_UP)
        q2 = send(g2 + o[8:12], "row", Y_FAR)
        q3 = send(g3 + o[12:], "row", Y_DOWN)
        (flipped,) = bar(keep + h)
        flipped_back = flip(flipped)
        last = send(g0[2:] + o[2:4] + q1[2:] + q2[2:] + q3[2:], "row", X_HI)
        (own,) = bar(g0[:2] + o[:2] + q1[:2] + q2[:2] + q3[:2] + last)
        return own, flipped, flipped_back, t0

    y0 = vectors.reshape(vecs, -1, bs).transpose(1, 0, 2)

    def step(k, carry):
        before, now, flipping, scale, base = carry
        own, flipped, back, now_flipped = apply_hamiltonian(
            now, flip(flipping), base, lambda x, y: x * scale + y
        )
        later = (own + back - center * now) / half_width
        later = jnp.where(k == 0, later, 2.0 * later - before)
        base = (flipped - center * now_flipped) / half_width
        return now, later, own, 1.0 / half_width, base

    start = (y0, y0, y0, jnp.ones((), f32), jnp.zeros_like(y0))
    y2 = lax.fori_loop(0, 2, step, start)[1]
    return y2.transpose(1, 0, 2).reshape(vectors.shape)


def solution(mesh):
    placed = (
        P(None, ("col", "row")),
        P("row", "col", None, None, None),
        P("row", "col", None),
        P("row", "col", None),
        P("row", "col"),
        P(),
        P(),
    )
    return jax.shard_map(
        body, mesh=mesh, in_specs=placed, out_specs=P(None, ("col", "row")), check_vma=False
    )
```
